32 devices in a mesh: aa: 8 (over z, x), ba: 4 (over y, core).
Axes of the slice: x: 2, y: 2, z: 4, core: 2. Of those that a mesh axis runs over, the one named last changes fastest.
Arguments:
- patches: bfloat16 [8, 64, 512], P('ba'), may hold values from -6 to 6
- token_first: bfloat16 [8, 64, 256], P('aa'), may hold values from -0.75 to 0.75
- token_second: bfloat16 [8, 64, 256], P('aa'), may hold values from -0.375 to 0.375
- channel_first: bfloat16 [8, 512, 2048], P('aa'), may hold values from -0.25 to 0.25
- channel_second: bfloat16 [8, 2048, 512], P('aa'), may hold values from -0.1875 to 0.1875
- gains: float32 [8, 2, 512], P('aa'), may hold values from 0.25 to 1.75
- final_gain: float32 [512], replicated, may hold values from 0.25 to 1.75
- head_weight: bfloat16 [512, 1000], replicated, may hold values from -2 to 2
- depths: int32 [16, 2], replicated, may hold values from 1 to 4
- widths: int32 [16, 8], replicated, may hold values from 1 to 4
- labels: int32 [8], P('ba'), may hold values from 0 to 999
Outputs:
- losses: float32 [16], replicated
The draws below stay inside these ranges and needn't reach their ends.
All inputs are finite; a program needn't handle non-finite values.
Results may differ from the reference program's by a relative error of at most 0.0012.
Values may be sent and summed in bfloat16 or wider, within the bound.
A program may use at most 64 MiB of HBM per device.

```python
import jax
import jax.numpy as jnp
from jax import lax

D = 512
DS = 256
DC = 2048
CLASSES = 1000
S = 64
UNIT = 4
CAND = 16
SECTIONS = 8
UNITS = 2
IMAGES = 8
N_AA = 8


def place_ends(result, stream_key, least, largest):
    index_at = [jax.random.randint(jax.random.fold_in(stream_key, axis), (), 0, length) for axis, length in enumerate(result.shape)]
    main_axis = result.shape.index(max(result.shape))
    beside = index_at[:main_axis] + [(index_at[main_axis] + 1) % result.shape[main_axis]] + index_at[main_axis + 1:]
    return result.at[tuple(index_at)].set(least).at[tuple(beside)].set(largest)


def block_scale(key, shape, split, least, top_value):
    def one(position, shards_of):
        heights = jax.random.uniform(jax.random.fold_in(jax.random.fold_in(key, 6), position), (shards_of,), jnp.float32, least / len(split), top_value / len(split))
        return jnp.repeat(jnp.exp(heights), shape[position] // shards_of).reshape((-1,) + (1,) * (len(shape) - position - 1))

    level = one(*split[0])
    for cut in split[1:]:
        level = level * one(*cut)
    return level


def scatter_about(stream_key, dims, deviation, bound, cuts=(), dtype=jnp.bfloat16):
    entries = deviation * jax.random.normal(stream_key, dims, jnp.float32)
    if cuts:
        entries = entries * block_scale(stream_key, dims, cuts, -0.22, 0.18)
    return jnp.clip(entries, -bound, bound).astype(dtype)


def setup_inputs(seed: int = 0) -> dict:
    streams_of = jax.random.split(jax.random.key(seed), 12)
    patches = scatter_about(streams_of[0], (IMAGES, S, D), 1.0, 6.0, ((0, 4),))
    token_first = scatter_about(streams_of[1], (SECTIONS, S, DS), S ** -0.5, 0.75, ((0, 8),))
    token_second = scatter_about(streams_of[2], (SECTIONS, S, DS), DS ** -0.5, 0.375, ((0, 8),))
    channel_first = scatter_about(streams_of[3], (SECTIONS, D, DC), D ** -0.5, 0.25, ((0, 8),))
    channel_second = scatter_about(streams_of[4], (SECTIONS, DC, D), (DC // 2) ** -0.5, 0.1875, ((0, 8),))
    gains = jnp.clip(1.0 + 0.15 * jax.random.normal(streams_of[5], (SECTIONS, 2, D), jnp.float32), 0.25, 1.75)
    final_gain = jnp.clip(1.0 + 0.15 * jax.random.normal(streams_of[6], (D,), jnp.float32), 0.25, 1.75)
    head_weight = scatter_about(streams_of[7], (D, CLASSES), (max(D // 64, 1)) ** -0.5, 2.0)
    depths = place_ends(jax.random.randint(streams_of[8], (CAND, UNITS), 1, 5), jax.random.fold_in(streams_of[8], 1), 1, 4).astype(jnp.int32)
    widths = place_ends(jax.random.randint(streams_of[9], (CAND, SECTIONS), 1, 5), jax.random.fold_in(streams_of[9], 1), 1, 4).astype(jnp.int32)
    labels = place_ends(jax.random.randint(streams_of[10], (IMAGES,), 0, CLASSES), jax.random.fold_in(streams_of[10], 1), 0, CLASSES - 1).astype(jnp.int32)
    return dict(patches=patches, token_first=token_first, token_second=token_second, channel_first=channel_first, channel_second=channel_second, gains=gains, final_gain=final_gain, head_weight=head_weight, depths=depths, widths=widths, labels=labels)


def layer_norm(values, gain):
    center = values - lax.optimization_barrier(jnp.mean(values, axis=-1, keepdims=True))
    spread = lax.optimization_barrier(jnp.mean(center * center, axis=-1, keepdims=True))
    return center * lax.rsqrt(spread + 1e-06) * gain

def mixer_block(state, token_first_weight, token_second_weight, channel_one, channel_two, gain_pair, width):
    floats = state.astype(jnp.float32)
    normalized_input = layer_norm(floats, gain_pair[0]).astype(jnp.bfloat16)
    token_before_mixing = jnp.einsum('gtc,tp->gpc', normalized_input.astype(jnp.float32), token_first_weight.astype(jnp.float32))
    token_mixing_hidden = jax.nn.gelu(token_before_mixing, approximate=True).astype(jnp.bfloat16)
    token_portion = jnp.einsum('hcx,mc->hmx', token_mixing_hidden.astype(jnp.float32), token_second_weight.astype(jnp.float32))
    mixed = floats + token_portion
    second = layer_norm(mixed, gain_pair[1]).astype(jnp.bfloat16)
    rows = second.reshape(-1, D)
    channel_pre = jnp.dot(rows, channel_one, preferred_element_type=jnp.float32)
    lanes = jnp.arange(DC).astype(jnp.int32)
    keep = lanes < width * (DC // 4)
    channel_hidden = jnp.where(keep[None, :], jax.nn.gelu(channel_pre, approximate=True), 0.0).astype(jnp.bfloat16)
    channel_portion = jnp.dot(channel_hidden, channel_two, preferred_element_type=jnp.float32)
    return (mixed + channel_portion.reshape(mixed.shape)).astype(jnp.bfloat16)

def head_loss(state, final_gain, head_weight, labels):
    normalized_input = layer_norm(state.astype(jnp.float32), final_gain)
    pooled = lax.optimization_barrier(jnp.mean(normalized_input, axis=1)).astype(jnp.bfloat16)
    logits = jnp.dot(pooled, head_weight, preferred_element_type=jnp.float32)
    total = jax.nn.logsumexp(logits, axis=-1)
    classes = jnp.arange(CLASSES).astype(jnp.int32)
    picked = lax.optimization_barrier(jnp.sum(jnp.where(classes[None, :] == labels[:, None], logits, 0.0), axis=-1))
    return jnp.sum(total - picked)

def reference(patches, token_first, token_second, channel_first, channel_second, gains, final_gain, head_weight, depths, widths, labels):

    def one_candidate(pair):
        depth_choice_row, width_row = pair
        state = patches
        for section in range(N_AA):
            updated = mixer_block(state, token_first[section], token_second[section], channel_first[section], channel_second[section], gains[section], width_row[section])
            active = section % UNIT < depth_choice_row[section // UNIT]
            state = jnp.where(active, updated, state)
        return head_loss(state, final_gain, head_weight, labels)
    return lax.map(one_candidate, (depths, widths))
```

```python
import functools

import jax
import jax.numpy as jnp
from jax import lax
from jax.experimental import pallas as pl
from jax.experimental.pallas import tpu as pltpu
from jax.sharding import PartitionSpec as P

UNIT = 4
QUARTERS = 4
TEAM = 4
MESH = pl.DeviceIdType.MESH
GELU_A = 0.7978845608028654
GELU_B = 0.044715 * GELU_A


def layer_norm(values, gain):
    center = values - jnp.mean(values, axis=-1, keepdims=True)
    spread = jnp.mean(center * center, axis=-1, keepdims=True)
    return center * lax.rsqrt(spread + 1e-06) * gain


def gelu(x, half):
    bent = jnp.tanh(x * (GELU_A + GELU_B * (x * x)))
    scaled = x * half
    return scaled + scaled * bent


def dot(a, b):
    return jnp.dot(a, b, preferred_element_type=jnp.float32)


def token_mix(floats, gain, token_one_t, token_two):
    model = floats[0].shape[1]
    normed = jnp.concatenate(
        [layer_norm(value, gain).astype(jnp.bfloat16) for value in floats], axis=1
    )
    hidden = gelu(dot(token_one_t, normed), 0.5).astype(jnp.bfloat16)
    part = dot(token_two, hidden)
    return jnp.concatenate(
        [
            value + part[:, unit * model : (unit + 1) * model]
            for unit, value in enumerate(floats)
        ],
        axis=0,
    )


def kernel(
    sections,
    shards,
    depths,
    widths,
    labels,
    patches,
    gains,
    token_first,
    token_second,
    channel_first,
    channel_second,
    final_gain,
    head_weight_t,
    out,
    inbox,
    outbox,
    options,
    token_one,
    token_two,
    token_one_t,
    channel_one,
    channel_two,
    gain_pair,
    head,
    pooled,
    share,
    landing,
    load_sem,
    small_send,
    small_recv,
    weight_send,
    weight_recv,
    state_send,
    state_recv,
    share_send,
    landing_sem,
):
    section = lax.axis_index("aa")
    shard = lax.axis_index("ba")
    pair = section // 2
    side = section % 2
    pairs = sections // 2
    last = pairs - 1
    images, patch_count, model = patches.shape
    candidates = depths.shape[1]
    per = candidates // 2
    slots = per * images
    hidden_units = channel_first.shape[2]
    quarter = hidden_units // QUARTERS
    partner = section + 1 - 2 * side
    rank = shard % TEAM
    team = shard - rank
    beside = team + rank + 1 - 2 * (rank % 2)
    across = team + (rank + 2) % TEAM

    loads = [
        pltpu.make_async_copy(source.at[0], target.at[side], load_sem.at[index])
        for index, (source, target) in enumerate(
            (
                (token_first, token_one),
                (token_second, token_two),
                (channel_first, channel_one),
                (channel_second, channel_two),
                (gains, gain_pair),
            )
        )
    ]
    head_load = pltpu.make_async_copy(head_weight_t, head, load_sem.at[5])
    for load in loads:
        load.start()

    @pl.when(pair == last)
    def _():
        head_load.start()

    barrier = pltpu.get_barrier_semaphore()

    def greet(aa, ba):
        pl.semaphore_signal(barrier, inc=1, device_id=(aa, ba), device_id_type=MESH)

    @pl.when(section == 1)
    def _():
        greet(0, shard)

    @pl.when(pair == 1)
    def _():
        greet(1, shard)

    @pl.when(pair > 0)
    def _():
        greet(partner, shard)
        greet(section, beside)
        greet(section, across)

    @pl.when(pair > 1)
    def _():
        greet(section - 2, shard)

    def greet_last(target, carry):
        aa, ba = 2 * last + target // shards, target % shards

        @pl.when(jnp.logical_or(aa != section, ba != shard))
        def _():
            greet(aa, ba)

        return carry

    lax.fori_loop(0, 2 * shards, greet_last, 0)

    def wait_greetings():
        @pl.when(section == 0)
        def _():
            pl.semaphore_wait(barrier, 1)

        @pl.when(section == 1)
        def _():
            pl.semaphore_wait(barrier, 2)

        @pl.when(jnp.logical_and(pair > 0, pair < last))
        def _():
            pl.semaphore_wait(barrier, 4)

        @pl.when(pair == last)
        def _():
            pl.semaphore_wait(barrier, 3 + sections * shards - 1)

    wait_greetings()

    def state_copy(source, target, aa):
        return pltpu.make_async_remote_copy(
            src_ref=outbox.at[source],
            dst_ref=inbox.at[target],
            send_sem=state_send.at[source],
            recv_sem=state_recv.at[target],
            device_id=(aa, shard),
            device_id_type=MESH,
        )

    def arrived(slot):
        state_copy(slot, slot, section).wait_recv()

    @pl.when(section == 0)
    def _():
        for load in loads:
            load.wait()
        floats = [patches[image].astype(jnp.float32) for image in range(images)]
        mixed = token_mix(floats, gain_pair[0, 0:1, :], token_one[0].T, token_two[0])
        second = layer_norm(mixed, gain_pair[0, 1:2, :]).astype(jnp.bfloat16)
        total = mixed
        for width in range(QUARTERS):
            cut = slice(width * quarter, (width + 1) * quarter)
            hidden = gelu(dot(second, channel_one[0, :, cut]), 0.5)
            total = total + dot(hidden.astype(jnp.bfloat16), channel_two[0, cut, :])
            rounded = total.astype(jnp.bfloat16)
            for image in range(images):
                slot = image * QUARTERS + width
                outbox[slot] = rounded[image * patch_count : (image + 1) * patch_count]
        for slot in range(images * QUARTERS):
            state_copy(slot, slot, 1).start()
        for slot in range(images * QUARTERS):
            state_copy(slot, slot, 1).wait_send()

    @pl.when(section == 1)
    def _():
        for load in loads:
            load.wait()

        def image_step(image, carry):
            base = image * QUARTERS
            for width in range(QUARTERS):
                arrived(base + width)
            states = [inbox[base + width] for width in range(QUARTERS)]
            floats = [state.astype(jnp.float32) for state in states]
            mixed = token_mix(
                floats, gain_pair[1, 0:1, :], token_one[1].T, token_two[1]
            )
            second = layer_norm(mixed, gain_pair[1, 1:2, :]).astype(jnp.bfloat16)
            total = mixed
            for first in range(QUARTERS):
                options[first] = states[first]
            for width in range(QUARTERS):
                cut = slice(width * quarter, (width + 1) * quarter)
                hidden = gelu(dot(second, channel_one[1, :, cut]), 0.5)
                total = total + dot(hidden.astype(jnp.bfloat16), channel_two[1, cut, :])
                rounded = total.astype(jnp.bfloat16)
                for first in range(QUARTERS):
                    options[(width + 1) * QUARTERS + first] = rounded[
                        first * patch_count : (first + 1) * patch_count
                    ]

            def pick(index, carry):
                for parity in range(2):
                    candidate = 2 * index + parity
                    active = 1 < depths[0, candidate]
                    chosen = jnp.where(active, widths[1, candidate], 0)
                    row = chosen * QUARTERS + jnp.maximum(widths[0, candidate], 1) - 1
                    slot = image * per + index
                    outbox[parity * slots + slot] = options[row]
                    state_copy(parity * slots + slot, slot, 2 + parity).start()
                return carry

            lax.fori_loop(0, per, pick, 0)
            return carry

        lax.fori_loop(0, images, image_step, 0)

        def drain(index, carry):
            state_copy(index, index % slots, 2).wait_send()
            return carry

        lax.fori_loop(0, 2 * slots, drain, 0)

    rounds = QUARTERS
    piece = quarter // TEAM

    def weight_copy(part, from_input, kind, turn, owner, aa, ba, which):
        start = turn * quarter + owner * piece
        cut = pl.ds(pl.multiple_of(start, piece), piece)
        if which == 0:
            ref = channel_first.at[0, :, cut] if from_input else channel_one.at[part, :, cut]
            target = channel_one.at[part, :, cut]
        else:
            ref = channel_second.at[0, cut, :] if from_input else channel_two.at[part, cut, :]
            target = channel_two.at[part, cut, :]
        return pltpu.make_async_remote_copy(
            src_ref=ref,
            dst_ref=target,
            send_sem=weight_send.at[kind, turn, which],
            recv_sem=weight_recv.at[owner, turn, which],
            device_id=(aa, ba),
            device_id_type=MESH,
        )

    other = 1 - side

    def small_copies(part):
        return [
            pltpu.make_async_remote_copy(
                src_ref=source.at[0],
                dst_ref=target.at[part],
                send_sem=small_send.at[index],
                recv_sem=small_recv.at[index],
                device_id=(partner, shard),
                device_id_type=MESH,
            )
            for index, (source, target) in enumerate(
                (
                    (token_first, token_one),
                    (token_second, token_two),
                    (gains, gain_pair),
                )
            )
        ]

    rank_beside = rank + 1 - 2 * (rank % 2)
    rank_across = (rank + 2) % TEAM
    rank_far = (rank_beside + 2) % TEAM

    def to_partner(turn, which):
        return weight_copy(side, True, 0, turn, rank, partner, shard, which)

    def to_across(turn, which):
        return weight_copy(other, False, 1, turn, rank, section, across, which)

    def to_beside(turn, which):
        return weight_copy(other, False, 2, turn, rank, section, beside, which)

    def to_beside_again(turn, which):
        return weight_copy(other, False, 3, turn, rank_across, section, beside, which)

    def from_owner(turn, owner, which):
        return weight_copy(other, False, 0, turn, owner, section, shard, which)

    def section_step(group, first, finish, parity, states):
        here = 2 * pair + parity
        floats = [state.astype(jnp.float32) for state in states]
        mixed = token_mix(
            floats, gain_pair[parity, 0:1, :], token_one_t[parity], token_two[parity]
        )
        second = layer_norm(mixed, gain_pair[parity, 1:2, :]).astype(jnp.bfloat16)
        pre = dot(second, channel_one[parity])
        lane = lax.broadcasted_iota(jnp.int32, (1, hidden_units), 1)
        parts = []
        actives = []
        for unit in range(group):
            candidate = 2 * ((first + unit) % per) + side
            actives.append(here % UNIT < depths[here // UNIT, candidate])
            half = jnp.where(lane < widths[here, candidate] * quarter, 0.5, 0.0)
            rows = slice(unit * patch_count, (unit + 1) * patch_count)
            parts.append(gelu(pre[rows], half).astype(jnp.bfloat16))
        hidden = jnp.concatenate(parts, axis=0)
        total = (mixed + dot(hidden, channel_two[parity])).astype(jnp.bfloat16)
        return [
            jnp.where(
                actives[unit],
                total[unit * patch_count : (unit + 1) * patch_count],
                states[unit],
            )
            for unit in range(group)
        ]

    def chunk(group, offset, index, carry):
        first = offset + index * group
        for unit in range(group):
            arrived(first + unit)

        def both(parity, carry):
            states = [inbox[first + unit] for unit in range(group)]
            updated = section_step(group, first, False, parity, states)
            for unit in range(group):
                outbox[first + unit] = updated[unit]

            @pl.when(parity == 0)
            def _():
                for unit in range(group):
                    inbox[first + unit] = updated[unit]

            return carry

        lax.fori_loop(0, 2, both, 0)

        @pl.when(pair < last)
        def _():
            for unit in range(group):
                state_copy(first + unit, first + unit, section + 2).start()

        @pl.when(pair == last)
        def _():
            for unit in range(group):
                final = layer_norm(
                    outbox[first + unit].astype(jnp.float32), final_gain[...]
                )
                pooled[pl.ds(first + unit, 1), :] = jnp.mean(
                    final, axis=0, keepdims=True
                )

        return carry

    @pl.when(pair > 0)
    def _():
        for copy in small_copies(side):
            copy.start()
        for turn in range(rounds):
            for which in range(2):
                to_partner(turn, which).start()
        for load in loads:
            load.wait()
        token_one_t[side] = token_one[side].T
        for copy in small_copies(other):
            copy.wait_recv()
        token_one_t[other] = token_one[other].T
        for turn in range(rounds):
            for which in range(2):
                from_owner(turn, rank, which).wait_recv()
                to_across(turn, which).start()
                to_beside(turn, which).start()
            for which in range(2):
                from_owner(turn, rank_across, which).wait_recv()
                to_beside_again(turn, which).start()
        for turn in range(rounds):
            for owner in (rank_beside, rank_far):
                for which in range(2):
                    from_owner(turn, owner, which).wait_recv()
        big = 4 if slots % 4 == 0 and slots >= 8 else 1
        small = 2 if big == 4 else 1
        tail = big if big > 1 else 0
        lax.fori_loop(
            0, (slots - tail) // big, functools.partial(chunk, big, 0), 0
        )
        if tail:
            lax.fori_loop(
                0, tail // small, functools.partial(chunk, small, slots - tail), 0
            )
        for copy in small_copies(side):
            copy.wait_send()
        for turn in range(rounds):
            for copy in (to_partner, to_across, to_beside, to_beside_again):
                for which in range(2):
                    copy(turn, which).wait_send()

    @pl.when(jnp.logical_and(pair > 0, pair < last))
    def _():
        def drain(slot, carry):
            state_copy(slot, slot, section + 2).wait_send()
            return carry

        lax.fori_loop(0, slots, drain, 0)

    def tell(aa, ba):
        mine = side * shards + shard
        return pltpu.make_async_remote_copy(
            src_ref=share,
            dst_ref=landing.at[mine],
            send_sem=share_send.at[aa * shards + ba],
            recv_sem=landing_sem.at[mine],
            device_id=(aa, ba),
            device_id_type=MESH,
        )

    def each_other(act):
        def visit(target, carry):
            aa, ba = target // shards, target % shards

            @pl.when(jnp.logical_or(aa != section, ba != shard))
            def _():
                act(tell(aa, ba))

            return carry

        lax.fori_loop(0, sections * shards, visit, 0)

    @pl.when(pair == last)
    def _():
        head_load.wait()
        logits = lax.dot_general(
            pooled[...].astype(jnp.bfloat16),
            head[...],
            (((1,), (1,)), ((), ())),
            preferred_element_type=jnp.float32,
        )
        top = jnp.max(logits, axis=-1, keepdims=True)
        total = top + jnp.log(jnp.sum(jnp.exp(logits - top), axis=-1, keepdims=True))
        rows = lax.broadcasted_iota(jnp.int32, logits.shape, 0)
        classes = lax.broadcasted_iota(jnp.int32, logits.shape, 1)
        wanted = jnp.full(logits.shape, labels[0], jnp.int32)
        for image in range(1, images):
            wanted = jnp.where(rows >= image * per, labels[image], wanted)
        picked = jnp.sum(
            jnp.where(classes == wanted, logits, 0.0), axis=-1, keepdims=True
        )
        losses = total - picked
        summed = losses[:per]
        for image in range(1, images):
            summed = summed + losses[image * per : (image + 1) * per]
        lanes = out.shape[1]
        rows = lax.broadcasted_iota(jnp.int32, (per, lanes), 0)
        cols = lax.broadcasted_iota(jnp.int32, (per, lanes), 1)
        spread = jnp.broadcast_to(summed, (per, lanes))
        line = jnp.sum(
            jnp.where(2 * rows + side == cols, spread, 0.0), axis=0, keepdims=True
        )
        share[...] = line
        landing[side * shards + shard] = line
        each_other(lambda copy: copy.start())
        each_other(lambda copy: copy.wait_send())

    for origin in range(2 * shards):
        aa, ba = 2 * last + origin // shards, origin % shards

        @pl.when(jnp.logical_or(section != aa, shard != ba))
        def _():
            pltpu.make_async_remote_copy(
                src_ref=share,
                dst_ref=landing.at[origin],
                send_sem=share_send.at[0],
                recv_sem=landing_sem.at[origin],
                device_id=(aa, ba),
                device_id_type=MESH,
            ).wait_recv()

    result = landing[0]
    for origin in range(1, 2 * shards):
        result = result + landing[origin]
    out[...] = result


def solution(mesh):
    sections, shards = mesh.shape["aa"], mesh.shape["ba"]

    def local(
        patches,
        token_first,
        token_second,
        channel_first,
        channel_second,
        gains,
        final_gain,
        head_weight,
        depths,
        widths,
        labels,
    ):
        images, patch_count, model = patches.shape
        candidates = depths.shape[0]
        slots = candidates // 2 * images
        lanes = pl.cdiv(candidates, 128) * 128
        smem = pl.BlockSpec(memory_space=pltpu.SMEM)
        vmem = pl.BlockSpec(memory_space=pltpu.VMEM)
        hbm = pl.BlockSpec(memory_space=pl.ANY)
        bf16 = jnp.bfloat16
        dma = pltpu.SemaphoreType.DMA
        line = pl.pallas_call(
            functools.partial(kernel, sections, shards),
            out_shape=jax.ShapeDtypeStruct((1, lanes), jnp.float32),
            in_specs=[smem] * 3 + [vmem] + [hbm] * 5 + [vmem] + [hbm],
            out_specs=vmem,
            scratch_shapes=[
                pltpu.VMEM((slots, patch_count, model), bf16),
                pltpu.VMEM((2 * slots, patch_count, model), bf16),
                pltpu.VMEM(((QUARTERS + 1) * QUARTERS, patch_count, model), bf16),
                pltpu.VMEM((2,) + token_first.shape[1:], bf16),
                pltpu.VMEM((2,) + token_second.shape[1:], bf16),
                pltpu.VMEM((2, token_first.shape[2], patch_count), bf16),
                pltpu.VMEM((2,) + channel_first.shape[1:], bf16),
                pltpu.VMEM((2,) + channel_second.shape[1:], bf16),
                pltpu.VMEM((2,) + gains.shape[1:], jnp.float32),
                pltpu.VMEM(head_weight.shape[::-1], bf16),
                pltpu.VMEM((slots, model), jnp.float32),
                pltpu.VMEM((1, lanes), jnp.float32),
                pltpu.VMEM((2 * shards, 1, lanes), jnp.float32),
                dma((6,)),
                dma((3,)),
                dma((3,)),
                dma((4, QUARTERS, 2)),
                dma((TEAM, QUARTERS, 2)),
                dma((2 * slots,)),
                dma((slots,)),
                dma((sections * shards,)),
                dma((2 * shards,)),
            ],
            compiler_params=pltpu.CompilerParams(
                collective_id=0,
                has_side_effects=True,
                vmem_limit_bytes=40 * 1024 * 1024,
            ),
        )(
            depths.T,
            widths.T,
            labels,
            patches,
            gains,
            token_first,
            token_second,
            channel_first,
            channel_second,
            final_gain[None, :],
            head_weight.T,
        )
        return line[0, :candidates]

    return jax.shard_map(
        local,
        mesh=mesh,
        in_specs=(
            P("ba", None, None),
            P("aa", None, None),
            P("aa", None, None),
            P("aa", None, None),
            P("aa", None, None),
            P("aa", None, None),
            P(),
            P(),
            P(),
            P(),
            P("ba"),
        ),
        out_specs=P(),
        check_vma=False,
    )
```

```python
import functools

import jax
import jax.numpy as jnp
from jax import lax
from jax.experimental import pallas as pl
from jax.experimental.pallas import tpu as pltpu
from jax.sharding import PartitionSpec as P

UNIT = 4
QUARTERS = 4
TEAM = 4
MESH = pl.DeviceIdType.MESH
GELU_A = 0.7978845608028654
GELU_B = 0.044715 * GELU_A


def layer_norm(values, gain):
    center = values - jnp.mean(values, axis=-1, keepdims=True)
    spread = jnp.mean(center * center, axis=-1, keepdims=True)
    return center * lax.rsqrt(spread + 1e-06) * gain


def gelu(x, half):
    bent = jnp.tanh(x * (GELU_A + GELU_B * (x * x)))
    scaled = x * half
    return scaled + scaled * bent


def dot(a, b):
    return jnp.dot(a, b, preferred_element_type=jnp.float32)


def token_mix(floats, gain, token_one_t, token_two):
    model = floats[0].shape[1]
    normed = jnp.concatenate(
        [layer_norm(value, gain).astype(jnp.bfloat16) for value in floats], axis=1
    )
    hidden = gelu(dot(token_one_t, normed), 0.5).astype(jnp.bfloat16)
    part = dot(token_two, hidden)
    return jnp.concatenate(
        [
            value + part[:, unit * model : (unit + 1) * model]
            for unit, value in enumerate(floats)
        ],
        axis=0,
    )


def kernel(
    sections,
    shards,
    depths,
    widths,
    labels,
    patches,
    gains,
    token_first,
    token_second,
    channel_first,
    channel_second,
    final_gain,
    head_weight_t,
    out,
    inbox,
    outbox,
    options,
    token_one,
    token_two,
    token_one_t,
    channel_one,
    channel_two,
    gain_pair,
    head,
    pooled,
    share,
    landing,
    answer,
    load_sem,
    small_send,
    small_recv,
    weight_send,
    weight_recv,
    state_send,
    state_recv,
    share_send,
    landing_sem,
    answer_send,
    answer_recv,
):
    section = lax.axis_index("aa")
    shard = lax.axis_index("ba")
    pair = section // 2
    side = section % 2
    pairs = sections // 2
    last = pairs - 1
    images, patch_count, model = patches.shape
    candidates = depths.shape[1]
    per = candidates // 2
    slots = per * images
    hidden_units = channel_first.shape[2]
    quarter = hidden_units // QUARTERS
    partner = section + 1 - 2 * side
    rank = shard % TEAM
    team = shard - rank
    beside = team + rank + 1 - 2 * (rank % 2)
    across = team + (rank + 2) % TEAM

    loads = [
        pltpu.make_async_copy(source.at[0], target.at[side], load_sem.at[index])
        for index, (source, target) in enumerate(
            (
                (token_first, token_one),
                (token_second, token_two),
                (channel_first, channel_one),
                (channel_second, channel_two),
                (gains, gain_pair),
            )
        )
    ]
    head_load = pltpu.make_async_copy(head_weight_t, head, load_sem.at[5])
    for load in loads:
        load.start()

    @pl.when(pair == last)
    def _():
        head_load.start()

    barrier = pltpu.get_barrier_semaphore()

    def greet(aa, ba):
        pl.semaphore_signal(barrier, inc=1, device_id=(aa, ba), device_id_type=MESH)

    @pl.when(pair == 0)
    def _():
        greet(partner, shard)

    @pl.when(pair == 1)
    def _():
        greet(side, shard)

    @pl.when(pair > 0)
    def _():
        greet(partner, shard)
        greet(section, beside)
        greet(section, across)

    @pl.when(pair > 1)
    def _():
        greet(section - 2, shard)

    @pl.when(pair < last)
    def _():
        greet(2 * last + side, shard)

    @pl.when(pair == last)
    def _():
        def greet_last(target, carry):
            aa, ba = 2 * last + target // shards, target % shards

            @pl.when(jnp.logical_or(aa != section, ba != shard))
            def _():
                greet(aa, ba)

            return carry

        lax.fori_loop(0, 2 * shards, greet_last, 0)

    @pl.when(pair == 0)
    def _():
        pl.semaphore_wait(barrier, 2)

    @pl.when(jnp.logical_and(pair > 0, pair < last))
    def _():
        pl.semaphore_wait(barrier, 4)

    @pl.when(pair == last)
    def _():
        pl.semaphore_wait(barrier, 3 + 2 * shards - 1 + last)

    def state_copy(source, target, aa):
        return pltpu.make_async_remote_copy(
            src_ref=outbox.at[source],
            dst_ref=inbox.at[target],
            send_sem=state_send.at[source],
            recv_sem=state_recv.at[target],
            device_id=(aa, shard),
            device_id_type=MESH,
        )

    def arrived(slot):
        state_copy(slot, slot, section).wait_recv()

    @pl.when(section == 0)
    def _():
        for load in loads:
            load.wait()
        floats = [patches[image].astype(jnp.float32) for image in range(images)]
        mixed = token_mix(floats, gain_pair[0, 0:1, :], token_one[0].T, token_two[0])
        second = layer_norm(mixed, gain_pair[0, 1:2, :]).astype(jnp.bfloat16)
        total = mixed
        for width in range(QUARTERS):
            cut = slice(width * quarter, (width + 1) * quarter)
            hidden = gelu(dot(second, channel_one[0, :, cut]), 0.5)
            total = total + dot(hidden.astype(jnp.bfloat16), channel_two[0, cut, :])
            rounded = total.astype(jnp.bfloat16)
            for image in range(images):
                slot = image * QUARTERS + width
                outbox[slot] = rounded[image * patch_count : (image + 1) * patch_count]
        for slot in range(images * QUARTERS):
            state_copy(slot, slot, 1).start()

        def relay(slot):
            return pltpu.make_async_remote_copy(
                src_ref=inbox.at[slot],
                dst_ref=inbox.at[slot],
                send_sem=state_send.at[slots + slot],
                recv_sem=state_recv.at[slot],
                device_id=(2, shard),
                device_id_type=MESH,
            )

        def pass_on(slot, carry):
            arrived(slot)
            relay(slot).start()
            return carry

        def drain(slot, carry):
            relay(slot).wait_send()
            return carry

        lax.fori_loop(0, slots, pass_on, 0)
        lax.fori_loop(0, slots, drain, 0)
        for slot in range(images * QUARTERS):
            state_copy(slot, slot, 1).wait_send()

    @pl.when(section == 1)
    def _():
        for load in loads:
            load.wait()

        def image_step(image, carry):
            base = image * QUARTERS
            for width in range(QUARTERS):
                arrived(base + width)
            states = [inbox[base + width] for width in range(QUARTERS)]
            floats = [state.astype(jnp.float32) for state in states]
            mixed = token_mix(
                floats, gain_pair[1, 0:1, :], token_one[1].T, token_two[1]
            )
            second = layer_norm(mixed, gain_pair[1, 1:2, :]).astype(jnp.bfloat16)
            total = mixed
            for first in range(QUARTERS):
                options[first] = states[first]
            for width in range(QUARTERS):
                cut = slice(width * quarter, (width + 1) * quarter)
                hidden = gelu(dot(second, channel_one[1, :, cut]), 0.5)
                total = total + dot(hidden.astype(jnp.bfloat16), channel_two[1, cut, :])
                rounded = total.astype(jnp.bfloat16)
                for first in range(QUARTERS):
                    options[(width + 1) * QUARTERS + first] = rounded[
                        first * patch_count : (first + 1) * patch_count
                    ]

            def pick(index, carry):
                for parity in range(2):
                    candidate = 2 * index + parity
                    active = 1 < depths[0, candidate]
                    chosen = jnp.where(active, widths[1, candidate], 0)
                    row = chosen * QUARTERS + jnp.maximum(widths[0, candidate], 1) - 1
                    slot = image * per + index
                    outbox[parity * slots + slot] = options[row]
                    state_copy(parity * slots + slot, slot, 3 * parity).start()
                return carry

            lax.fori_loop(0, per, pick, 0)
            return carry

        lax.fori_loop(0, images, image_step, 0)

        def drain(index, carry):
            state_copy(index, index % slots, 2).wait_send()
            return carry

        lax.fori_loop(0, 2 * slots, drain, 0)

    rounds = QUARTERS
    piece = quarter // TEAM

    def weight_copy(part, from_input, kind, turn, owner, aa, ba, which):
        start = turn * quarter + owner * piece
        cut = pl.ds(pl.multiple_of(start, piece), piece)
        if which == 0:
            ref = channel_first.at[0, :, cut] if from_input else channel_one.at[part, :, cut]
            target = channel_one.at[part, :, cut]
        else:
            ref = channel_second.at[0, cut, :] if from_input else channel_two.at[part, cut, :]
            target = channel_two.at[part, cut, :]
        return pltpu.make_async_remote_copy(
            src_ref=ref,
            dst_ref=target,
            send_sem=weight_send.at[kind, turn, which],
            recv_sem=weight_recv.at[owner, turn, which],
            device_id=(aa, ba),
            device_id_type=MESH,
        )

    other = 1 - side

    def small_copies(part):
        return [
            pltpu.make_async_remote_copy(
                src_ref=source.at[0],
                dst_ref=target.at[part],
                send_sem=small_send.at[index],
                recv_sem=small_recv.at[index],
                device_id=(partner, shard),
                device_id_type=MESH,
            )
            for index, (source, target) in enumerate(
                (
                    (token_first, token_one),
                    (token_second, token_two),
                    (gains, gain_pair),
                )
            )
        ]

    rank_beside = rank + 1 - 2 * (rank % 2)
    rank_across = (rank + 2) % TEAM
    rank_far = (rank_beside + 2) % TEAM

    def to_partner(turn, which):
        return weight_copy(side, True, 0, turn, rank, partner, shard, which)

    def to_across(turn, which):
        return weight_copy(other, False, 1, turn, rank, section, across, which)

    def to_beside(turn, which):
        return weight_copy(other, False, 2, turn, rank, section, beside, which)

    def to_beside_again(turn, which):
        return weight_copy(other, False, 3, turn, rank_across, section, beside, which)

    def from_owner(turn, owner, which):
        return weight_copy(other, False, 0, turn, owner, section, shard, which)

    def section_step(group, first, finish, parity, states):
        here = 2 * pair + parity
        floats = [state.astype(jnp.float32) for state in states]
        mixed = token_mix(
            floats, gain_pair[parity, 0:1, :], token_one_t[parity], token_two[parity]
        )
        second = layer_norm(mixed, gain_pair[parity, 1:2, :]).astype(jnp.bfloat16)
        pre = dot(second, channel_one[parity])
        lane = lax.broadcasted_iota(jnp.int32, (1, hidden_units), 1)
        parts = []
        actives = []
        for unit in range(group):
            candidate = 2 * ((first + unit) % per) + side
            actives.append(here % UNIT < depths[here // UNIT, candidate])
            half = jnp.where(lane < widths[here, candidate] * quarter, 0.5, 0.0)
            rows = slice(unit * patch_count, (unit + 1) * patch_count)
            parts.append(gelu(pre[rows], half).astype(jnp.bfloat16))
        hidden = jnp.concatenate(parts, axis=0)
        total = (mixed + dot(hidden, channel_two[parity])).astype(jnp.bfloat16)
        return [
            jnp.where(
                actives[unit],
                total[unit * patch_count : (unit + 1) * patch_count],
                states[unit],
            )
            for unit in range(group)
        ]

    def chunk(group, offset, index, carry):
        first = offset + index * group
        for unit in range(group):
            arrived(first + unit)

        def both(parity, carry):
            states = [inbox[first + unit] for unit in range(group)]
            updated = section_step(group, first, False, parity, states)
            for unit in range(group):
                outbox[first + unit] = updated[unit]

            @pl.when(parity == 0)
            def _():
                for unit in range(group):
                    inbox[first + unit] = updated[unit]

            return carry

        lax.fori_loop(0, 2, both, 0)

        @pl.when(pair < last)
        def _():
            for unit in range(group):
                state_copy(first + unit, first + unit, section + 2).start()

        @pl.when(pair == last)
        def _():
            for unit in range(group):
                final = layer_norm(
                    outbox[first + unit].astype(jnp.float32), final_gain[...]
                )
                pooled[pl.ds(first + unit, 1), :] = jnp.mean(
                    final, axis=0, keepdims=True
                )

        return carry

    @pl.when(pair > 0)
    def _():
        for copy in small_copies(side):
            copy.start()
        for turn in range(rounds):
            for which in range(2):
                to_partner(turn, which).start()
        for load in loads:
            load.wait()
        token_one_t[side] = token_one[side].T
        for copy in small_copies(other):
            copy.wait_recv()
        token_one_t[other] = token_one[other].T
        for turn in range(rounds):
            for which in range(2):
                from_owner(turn, rank, which).wait_recv()
                to_across(turn, which).start()
                to_beside(turn, which).start()
            for which in range(2):
                from_owner(turn, rank_across, which).wait_recv()
                to_beside_again(turn, which).start()
        for turn in range(rounds):
            for owner in (rank_beside, rank_far):
                for which in range(2):
                    from_owner(turn, owner, which).wait_recv()
        big = 4 if slots % 4 == 0 and slots >= 8 else 1
        small = 2 if big == 4 else 1
        tail = big if big > 1 else 0
        lax.fori_loop(
            0, (slots - tail) // big, functools.partial(chunk, big, 0), 0
        )
        if tail:
            lax.fori_loop(
                0, tail // small, functools.partial(chunk, small, slots - tail), 0
            )
        for copy in small_copies(side):
            copy.wait_send()
        for turn in range(rounds):
            for copy in (to_partner, to_across, to_beside, to_beside_again):
                for which in range(2):
                    copy(turn, which).wait_send()

    @pl.when(jnp.logical_and(pair > 0, pair < last))
    def _():
        def drain(slot, carry):
            state_copy(slot, slot, section + 2).wait_send()
            return carry

        lax.fori_loop(0, slots, drain, 0)

    def tell(aa, ba):
        mine = side * shards + shard
        return pltpu.make_async_remote_copy(
            src_ref=share,
            dst_ref=landing.at[mine],
            send_sem=share_send.at[(aa % 2) * shards + ba],
            recv_sem=landing_sem.at[mine],
            device_id=(aa, ba),
            device_id_type=MESH,
        )

    def each_other(act):
        def visit(target, carry):
            aa, ba = 2 * last + target // shards, target % shards

            @pl.when(jnp.logical_or(aa != section, ba != shard))
            def _():
                act(aa, ba, target)

            return carry

        lax.fori_loop(0, 2 * shards, visit, 0)

    def heard(aa, ba, origin):
        pltpu.make_async_remote_copy(
            src_ref=share,
            dst_ref=landing.at[origin],
            send_sem=share_send.at[0],
            recv_sem=landing_sem.at[origin],
            device_id=(aa, ba),
            device_id_type=MESH,
        ).wait_recv()

    def answer_copy(lower):
        return pltpu.make_async_remote_copy(
            src_ref=answer,
            dst_ref=answer,
            send_sem=answer_send.at[lower],
            recv_sem=answer_recv,
            device_id=(2 * lower + side, shard),
            device_id_type=MESH,
        )

    @pl.when(pair == last)
    def _():
        head_load.wait()
        logits = lax.dot_general(
            pooled[...].astype(jnp.bfloat16),
            head[...],
            (((1,), (1,)), ((), ())),
            preferred_element_type=jnp.float32,
        )
        top = jnp.max(logits, axis=-1, keepdims=True)
        total = top + jnp.log(jnp.sum(jnp.exp(logits - top), axis=-1, keepdims=True))
        rows = lax.broadcasted_iota(jnp.int32, logits.shape, 0)
        classes = lax.broadcasted_iota(jnp.int32, logits.shape, 1)
        wanted = jnp.full(logits.shape, labels[0], jnp.int32)
        for image in range(1, images):
            wanted = jnp.where(rows >= image * per, labels[image], wanted)
        picked = jnp.sum(
            jnp.where(classes == wanted, logits, 0.0), axis=-1, keepdims=True
        )
        losses = total - picked
        summed = losses[:per]
        for image in range(1, images):
            summed = summed + losses[image * per : (image + 1) * per]
        lanes = out.shape[1]
        rows = lax.broadcasted_iota(jnp.int32, (per, lanes), 0)
        cols = lax.broadcasted_iota(jnp.int32, (per, lanes), 1)
        spread = jnp.broadcast_to(summed, (per, lanes))
        line = jnp.sum(
            jnp.where(2 * rows + side == cols, spread, 0.0), axis=0, keepdims=True
        )
        share[...] = line
        landing[side * shards + shard] = line
        each_other(lambda aa, ba, target: tell(aa, ba).start())
        each_other(heard)
        result = landing[0]
        for origin in range(1, 2 * shards):
            result = result + landing[origin]
        answer[...] = result
        for lower in range(last):
            answer_copy(lower).start()
        each_other(lambda aa, ba, target: tell(aa, ba).wait_send())
        for lower in range(last):
            answer_copy(lower).wait_send()

    @pl.when(pair < last)
    def _():
        answer_copy(0).wait_recv()

    out[...] = answer[...]


def solution(mesh):
    sections, shards = mesh.shape["aa"], mesh.shape["ba"]

    def local(
        patches,
        token_first,
        token_second,
        channel_first,
        channel_second,
        gains,
        final_gain,
        head_weight,
        depths,
        widths,
        labels,
    ):
        images, patch_count, model = patches.shape
        candidates = depths.shape[0]
        slots = candidates // 2 * images
        lanes = pl.cdiv(candidates, 128) * 128
        smem = pl.BlockSpec(memory_space=pltpu.SMEM)
        vmem = pl.BlockSpec(memory_space=pltpu.VMEM)
        hbm = pl.BlockSpec(memory_space=pltpu.HBM)
        bf16 = jnp.bfloat16
        dma = pltpu.SemaphoreType.DMA
        line = pl.pallas_call(
            functools.partial(kernel, sections, shards),
            out_shape=jax.ShapeDtypeStruct((1, lanes), jnp.float32),
            in_specs=[smem] * 3 + [vmem] + [hbm] * 5 + [vmem] + [hbm],
            out_specs=vmem,
            scratch_shapes=[
                pltpu.VMEM((slots, patch_count, model), bf16),
                pltpu.VMEM((2 * slots, patch_count, model), bf16),
                pltpu.VMEM(((QUARTERS + 1) * QUARTERS, patch_count, model), bf16),
                pltpu.VMEM((2,) + token_first.shape[1:], bf16),
                pltpu.VMEM((2,) + token_second.shape[1:], bf16),
                pltpu.VMEM((2, token_first.shape[2], patch_count), bf16),
                pltpu.VMEM((2,) + channel_first.shape[1:], bf16),
                pltpu.VMEM((2,) + channel_second.shape[1:], bf16),
                pltpu.VMEM((2,) + gains.shape[1:], jnp.float32),
                pltpu.VMEM(head_weight.shape[::-1], bf16),
                pltpu.VMEM((slots, model), jnp.float32),
                pltpu.VMEM((1, lanes), jnp.float32),
                pltpu.VMEM((2 * shards, 1, lanes), jnp.float32),
                pltpu.VMEM((1, lanes), jnp.float32),
                dma((6,)),
                dma((3,)),
                dma((3,)),
                dma((4, QUARTERS, 2)),
                dma((TEAM, QUARTERS, 2)),
                dma((2 * slots,)),
                dma((slots,)),
                dma((2 * shards,)),
                dma((2 * shards,)),
                dma((sections // 2,)),
                dma(()),
            ],
            compiler_params=pltpu.CompilerParams(
                collective_id=0,
                has_side_effects=True,
                vmem_limit_bytes=58 * 1024 * 1024,
            ),
        )(
            depths.T,
            widths.T,
            labels,
            patches,
            gains,
            token_first,
            token_second,
            channel_first,
            channel_second,
            final_gain[None, :],
            head_weight.T,
        )
        return line[0, :candidates]

    return jax.shard_map(
        local,
        mesh=mesh,
        in_specs=(
            P("ba", None, None),
            P("aa", None, None),
            P("aa", None, None),
            P("aa", None, None),
            P("aa", None, None),
            P("aa", None, None),
            P(),
            P(),
            P(),
            P(),
            P("ba"),
        ),
        out_specs=P(),
        check_vma=False,
    )
```

```python
import functools

import jax
import jax.numpy as jnp
from jax import lax
from jax.experimental import pallas as pl
from jax.experimental.pallas import tpu as pltpu
from jax.sharding import PartitionSpec as P

UNIT = 4
QUARTERS = 4
TEAM = 4
MESH = pl.DeviceIdType.MESH
GELU_A = 0.7978845608028654
GELU_B = 0.044715 * GELU_A


def layer_norm(values, gain):
    center = values - jnp.mean(values, axis=-1, keepdims=True)
    spread = jnp.mean(center * center, axis=-1, keepdims=True)
    return center * lax.rsqrt(spread + 1e-06) * gain


def gelu(x, half):
    x = x.astype(jnp.bfloat16)
    bent = jnp.tanh(x * (jnp.bfloat16(GELU_A) + jnp.bfloat16(GELU_B) * (x * x)))
    scaled = x * half
    return scaled + scaled * bent


def dot(a, b):
    return jnp.dot(a, b, preferred_element_type=jnp.float32)


def token_mix(floats, gain, token_one_t, token_two):
    model = floats[0].shape[1]
    normed = jnp.concatenate(
        [layer_norm(value, gain).astype(jnp.bfloat16) for value in floats], axis=1
    )
    hidden = gelu(dot(token_one_t, normed), jnp.bfloat16(0.5))
    part = dot(token_two, hidden)
    return jnp.concatenate(
        [
            value + part[:, unit * model : (unit + 1) * model]
            for unit, value in enumerate(floats)
        ],
        axis=0,
    )


def kernel(
    sections,
    shards,
    depths,
    widths,
    labels,
    patches,
    gains,
    token_first,
    token_second,
    channel_first,
    channel_second,
    final_gain,
    head_weight_t,
    out,
    inbox,
    outbox,
    options,
    token_one,
    token_two,
    token_one_t,
    channel_one,
    channel_two,
    gain_pair,
    head,
    pooled,
    share,
    landing,
    load_sem,
    small_send,
    small_recv,
    weight_send,
    weight_recv,
    state_send,
    state_recv,
    share_send,
    landing_sem,
):
    section = lax.axis_index("aa")
    shard = lax.axis_index("ba")
    pair = section // 2
    side = section % 2
    pairs = sections // 2
    last = pairs - 1
    images, patch_count, model = patches.shape
    candidates = depths.shape[1]
    per = candidates // 2
    slots = per * images
    hidden_units = channel_first.shape[2]
    quarter = hidden_units // QUARTERS
    partner = section + 1 - 2 * side
    rank = shard % TEAM
    team = shard - rank
    beside = team + rank + 1 - 2 * (rank % 2)
    across = team + (rank + 2) % TEAM

    loads = [
        pltpu.make_async_copy(source.at[0], target.at[side], load_sem.at[index])
        for index, (source, target) in enumerate(
            (
                (token_first, token_one),
                (token_second, token_two),
                (channel_first, channel_one),
                (channel_second, channel_two),
                (gains, gain_pair),
            )
        )
    ]
    head_load = pltpu.make_async_copy(head_weight_t, head, load_sem.at[5])
    for load in loads:
        load.start()

    @pl.when(pair == last)
    def _():
        head_load.start()

    barrier = pltpu.get_barrier_semaphore()

    def greet(aa, ba):
        pl.semaphore_signal(barrier, inc=1, device_id=(aa, ba), device_id_type=MESH)

    @pl.when(pair == 0)
    def _():
        greet(partner, shard)

    @pl.when(pair == 1)
    def _():
        greet(side, shard)

    @pl.when(pair > 0)
    def _():
        greet(partner, shard)
        greet(section, beside)
        greet(section, across)

    @pl.when(pair > 1)
    def _():
        greet(section - 2, shard)

    def greet_last(target, carry):
        aa, ba = 2 * last + target // shards, target % shards

        @pl.when(jnp.logical_or(aa != section, ba != shard))
        def _():
            greet(aa, ba)

        return carry

    lax.fori_loop(0, 2 * shards, greet_last, 0)

    @pl.when(section == 1)
    def _():
        pl.semaphore_wait(barrier, 2)

    @pl.when(jnp.logical_and(pair > 0, pair < last))
    def _():
        pl.semaphore_wait(barrier, 4)

    @pl.when(pair == last)
    def _():
        pl.semaphore_wait(barrier, 3 + sections * shards - 1)

    def state_copy(source, target, aa):
        return pltpu.make_async_remote_copy(
            src_ref=outbox.at[source],
            dst_ref=inbox.at[target],
            send_sem=state_send.at[source],
            recv_sem=state_recv.at[target],
            device_id=(aa, shard),
            device_id_type=MESH,
        )

    def arrived(slot):
        state_copy(slot, slot, section).wait_recv()

    @pl.when(section == 0)
    def _():
        for load in loads:
            load.wait()
        floats = [patches[image].astype(jnp.float32) for image in range(images)]
        mixed = token_mix(floats, gain_pair[0, 0:1, :], token_one[0].T, token_two[0])
        second = layer_norm(mixed, gain_pair[0, 1:2, :]).astype(jnp.bfloat16)
        total = mixed
        for width in range(QUARTERS):
            cut = slice(width * quarter, (width + 1) * quarter)
            hidden = gelu(dot(second, channel_one[0, :, cut]), jnp.bfloat16(0.5))
            total = total + dot(hidden, channel_two[0, cut, :])
            rounded = total.astype(jnp.bfloat16)
            for image in range(images):
                slot = image * QUARTERS + width
                outbox[slot] = rounded[image * patch_count : (image + 1) * patch_count]
        pl.semaphore_wait(barrier, 2)
        for slot in range(images * QUARTERS):
            state_copy(slot, slot, 1).start()

        def relay(slot):
            return pltpu.make_async_remote_copy(
                src_ref=inbox.at[slot],
                dst_ref=inbox.at[slot],
                send_sem=state_send.at[slots + slot],
                recv_sem=state_recv.at[slot],
                device_id=(2, shard),
                device_id_type=MESH,
            )

        def pass_on(slot, carry):
            arrived(slot)
            relay(slot).start()
            return carry

        def drain(slot, carry):
            relay(slot).wait_send()
            return carry

        lax.fori_loop(0, slots, pass_on, 0)
        lax.fori_loop(0, slots, drain, 0)
        for slot in range(images * QUARTERS):
            state_copy(slot, slot, 1).wait_send()

    @pl.when(section == 1)
    def _():
        for load in loads:
            load.wait()

        def image_step(image, carry):
            base = image * QUARTERS
            for width in range(QUARTERS):
                arrived(base + width)
            states = [inbox[base + width] for width in range(QUARTERS)]
            floats = [state.astype(jnp.float32) for state in states]
            mixed = token_mix(
                floats, gain_pair[1, 0:1, :], token_one[1].T, token_two[1]
            )
            second = layer_norm(mixed, gain_pair[1, 1:2, :]).astype(jnp.bfloat16)
            total = mixed
            for first in range(QUARTERS):
                options[first] = states[first]
            for width in range(QUARTERS):
                cut = slice(width * quarter, (width + 1) * quarter)
                hidden = gelu(dot(second, channel_one[1, :, cut]), jnp.bfloat16(0.5))
                total = total + dot(hidden, channel_two[1, cut, :])
                rounded = total.astype(jnp.bfloat16)
                for first in range(QUARTERS):
                    options[(width + 1) * QUARTERS + first] = rounded[
                        first * patch_count : (first + 1) * patch_count
                    ]

            def pick(index, carry):
                for parity in range(2):
                    candidate = 2 * index + parity
                    active = 1 < depths[0, candidate]
                    chosen = jnp.where(active, widths[1, candidate], 0)
                    row = chosen * QUARTERS + jnp.maximum(widths[0, candidate], 1) - 1
                    slot = image * per + index
                    outbox[parity * slots + slot] = options[row]
                    state_copy(parity * slots + slot, slot, 3 * parity).start()
                return carry

            lax.fori_loop(0, per, pick, 0)
            return carry

        lax.fori_loop(0, images, image_step, 0)

        def drain(index, carry):
            state_copy(index, index % slots, 2).wait_send()
            return carry

        lax.fori_loop(0, 2 * slots, drain, 0)

    rounds = QUARTERS
    piece = quarter // TEAM

    def weight_copy(part, from_input, kind, turn, owner, aa, ba, which):
        start = turn * quarter + owner * piece
        cut = pl.ds(pl.multiple_of(start, piece), piece)
        if which == 0:
            ref = channel_first.at[0, :, cut] if from_input else channel_one.at[part, :, cut]
            target = channel_one.at[part, :, cut]
        else:
            ref = channel_second.at[0, cut, :] if from_input else channel_two.at[part, cut, :]
            target = channel_two.at[part, cut, :]
        return pltpu.make_async_remote_copy(
            src_ref=ref,
            dst_ref=target,
            send_sem=weight_send.at[kind, turn, which],
            recv_sem=weight_recv.at[owner, turn, which],
            device_id=(aa, ba),
            device_id_type=MESH,
        )

    other = 1 - side

    def small_copies(part):
        return [
            pltpu.make_async_remote_copy(
                src_ref=source.at[0],
                dst_ref=target.at[part],
                send_sem=small_send.at[index],
                recv_sem=small_recv.at[index],
                device_id=(partner, shard),
                device_id_type=MESH,
            )
            for index, (source, target) in enumerate(
                (
                    (token_first, token_one),
                    (token_second, token_two),
                    (gains, gain_pair),
                )
            )
        ]

    rank_beside = rank + 1 - 2 * (rank % 2)
    rank_across = (rank + 2) % TEAM
    rank_far = (rank_beside + 2) % TEAM

    def to_partner(turn, which):
        return weight_copy(side, True, 0, turn, rank, partner, shard, which)

    def to_across(turn, which):
        return weight_copy(other, False, 1, turn, rank, section, across, which)

    def to_beside(turn, which):
        return weight_copy(other, False, 2, turn, rank, section, beside, which)

    def to_beside_again(turn, which):
        return weight_copy(other, False, 3, turn, rank_across, section, beside, which)

    def from_owner(turn, owner, which):
        return weight_copy(other, False, 0, turn, owner, section, shard, which)

    def section_step(group, first, finish, parity, states):
        here = 2 * pair + parity
        floats = [state.astype(jnp.float32) for state in states]
        mixed = token_mix(
            floats, gain_pair[parity, 0:1, :], token_one_t[parity], token_two[parity]
        )
        second = layer_norm(mixed, gain_pair[parity, 1:2, :]).astype(jnp.bfloat16)
        pre = dot(second, channel_one[parity])
        lane = lax.broadcasted_iota(jnp.int32, (1, hidden_units), 1)
        parts = []
        actives = []
        for unit in range(group):
            candidate = 2 * ((first + unit) % per) + side
            actives.append(here % UNIT < depths[here // UNIT, candidate])
            half = jnp.where(lane < widths[here, candidate] * quarter, 0.5, 0.0).astype(
                jnp.bfloat16
            )
            rows = slice(unit * patch_count, (unit + 1) * patch_count)
            parts.append(gelu(pre[rows], half))
        hidden = jnp.concatenate(parts, axis=0)
        total = (mixed + dot(hidden, channel_two[parity])).astype(jnp.bfloat16)
        return [
            jnp.where(
                actives[unit],
                total[unit * patch_count : (unit + 1) * patch_count],
                states[unit],
            )
            for unit in range(group)
        ]

    def chunk(group, offset, index, carry):
        first = offset + index * group
        for unit in range(group):
            arrived(first + unit)

        def both(parity, carry):
            states = [inbox[first + unit] for unit in range(group)]
            updated = section_step(group, first, False, parity, states)
            for unit in range(group):
                outbox[first + unit] = updated[unit]

            @pl.when(parity == 0)
            def _():
                for unit in range(group):
                    inbox[first + unit] = updated[unit]

            return carry

        lax.fori_loop(0, 2, both, 0)

        @pl.when(pair < last)
        def _():
            for unit in range(group):
                state_copy(first + unit, first + unit, section + 2).start()

        @pl.when(pair == last)
        def _():
            for unit in range(group):
                final = layer_norm(
                    outbox[first + unit].astype(jnp.float32), final_gain[...]
                )
                pooled[pl.ds(first + unit, 1), :] = jnp.mean(
                    final, axis=0, keepdims=True
                )

        return carry

    @pl.when(pair > 0)
    def _():
        for copy in small_copies(side):
            copy.start()
        for turn in range(rounds):
            for which in range(2):
                to_partner(turn, which).start()
        for load in loads:
            load.wait()
        token_one_t[side] = token_one[side].T
        for copy in small_copies(other):
            copy.wait_recv()
        token_one_t[other] = token_one[other].T
        for turn in range(rounds):
            for which in range(2):
                from_owner(turn, rank, which).wait_recv()
                to_across(turn, which).start()
                to_beside(turn, which).start()
            for which in range(2):
                from_owner(turn, rank_across, which).wait_recv()
                to_beside_again(turn, which).start()
        for turn in range(rounds):
            for owner in (rank_beside, rank_far):
                for which in range(2):
                    from_owner(turn, owner, which).wait_recv()
        group = 2 if slots % 2 == 0 else 1
        lax.fori_loop(0, slots // group, functools.partial(chunk, group, 0), 0)
        for copy in small_copies(side):
            copy.wait_send()
        for turn in range(rounds):
            for copy in (to_partner, to_across, to_beside, to_beside_again):
                for which in range(2):
                    copy(turn, which).wait_send()

    @pl.when(jnp.logical_and(pair > 0, pair < last))
    def _():
        def drain(slot, carry):
            state_copy(slot, slot, section + 2).wait_send()
            return carry

        lax.fori_loop(0, slots, drain, 0)

    def tell(aa, ba):
        mine = side * shards + shard
        return pltpu.make_async_remote_copy(
            src_ref=share,
            dst_ref=landing.at[mine],
            send_sem=share_send.at[aa * shards + ba],
            recv_sem=landing_sem.at[mine],
            device_id=(aa, ba),
            device_id_type=MESH,
        )

    def each_other(act):
        def visit(target, carry):
            aa, ba = target // shards, target % shards

            @pl.when(jnp.logical_or(aa != section, ba != shard))
            def _():
                act(tell(aa, ba))

            return carry

        lax.fori_loop(0, sections * shards, visit, 0)

    def heard(aa, ba, origin):
        pltpu.make_async_remote_copy(
            src_ref=share,
            dst_ref=landing.at[origin],
            send_sem=share_send.at[0],
            recv_sem=landing_sem.at[origin],
            device_id=(aa, ba),
            device_id_type=MESH,
        ).wait_recv()

    @pl.when(pair == last)
    def _():
        head_load.wait()
        logits = lax.dot_general(
            pooled[...].astype(jnp.bfloat16),
            head[...],
            (((1,), (1,)), ((), ())),
            preferred_element_type=jnp.float32,
        )
        top = jnp.max(logits, axis=-1, keepdims=True)
        total = top + jnp.log(jnp.sum(jnp.exp(logits - top), axis=-1, keepdims=True))
        rows = lax.broadcasted_iota(jnp.int32, logits.shape, 0)
        classes = lax.broadcasted_iota(jnp.int32, logits.shape, 1)
        wanted = jnp.full(logits.shape, labels[0], jnp.int32)
        for image in range(1, images):
            wanted = jnp.where(rows >= image * per, labels[image], wanted)
        picked = jnp.sum(
            jnp.where(classes == wanted, logits, 0.0), axis=-1, keepdims=True
        )
        losses = total - picked
        summed = losses[:per]
        for image in range(1, images):
            summed = summed + losses[image * per : (image + 1) * per]
        lanes = out.shape[1]
        rows = lax.broadcasted_iota(jnp.int32, (per, lanes), 0)
        cols = lax.broadcasted_iota(jnp.int32, (per, lanes), 1)
        spread = jnp.broadcast_to(summed, (per, lanes))
        line = jnp.sum(
            jnp.where(2 * rows + side == cols, spread, 0.0), axis=0, keepdims=True
        )
        share[...] = line
        landing[side * shards + shard] = line
        each_other(lambda copy: copy.start())
        each_other(lambda copy: copy.wait_send())

    for origin in range(2 * shards):
        aa, ba = 2 * last + origin // shards, origin % shards

        @pl.when(jnp.logical_or(section != aa, shard != ba))
        def _():
            heard(aa, ba, origin)

    result = landing[0]
    for origin in range(1, 2 * shards):
        result = result + landing[origin]
    out[...] = result


def solution(mesh):
    sections, shards = mesh.shape["aa"], mesh.shape["ba"]

    def local(
        patches,
        token_first,
        token_second,
        channel_first,
        channel_second,
        gains,
        final_gain,
        head_weight,
        depths,
        widths,
        labels,
    ):
        images, patch_count, model = patches.shape
        candidates = depths.shape[0]
        slots = candidates // 2 * images
        lanes = pl.cdiv(candidates, 128) * 128
        smem = pl.BlockSpec(memory_space=pltpu.SMEM)
        vmem = pl.BlockSpec(memory_space=pltpu.VMEM)
        hbm = pl.BlockSpec(memory_space=pltpu.HBM)
        bf16 = jnp.bfloat16
        dma = pltpu.SemaphoreType.DMA
        line = pl.pallas_call(
            functools.partial(kernel, sections, shards),
            out_shape=jax.ShapeDtypeStruct((1, lanes), jnp.float32),
            in_specs=[smem] * 3 + [vmem] + [hbm] * 5 + [vmem] + [hbm],
            out_specs=vmem,
            scratch_shapes=[
                pltpu.VMEM((slots, patch_count, model), bf16),
                pltpu.VMEM((2 * slots, patch_count, model), bf16),
                pltpu.VMEM(((QUARTERS + 1) * QUARTERS, patch_count, model), bf16),
                pltpu.VMEM((2,) + token_first.shape[1:], bf16),
                pltpu.VMEM((2,) + token_second.shape[1:], bf16),
                pltpu.VMEM((2, token_first.shape[2], patch_count), bf16),
                pltpu.VMEM((2,) + channel_first.shape[1:], bf16),
                pltpu.VMEM((2,) + channel_second.shape[1:], bf16),
                pltpu.VMEM((2,) + gains.shape[1:], jnp.float32),
                pltpu.VMEM(head_weight.shape[::-1], bf16),
                pltpu.VMEM((slots, model), jnp.float32),
                pltpu.VMEM((1, lanes), jnp.float32),
                pltpu.VMEM((2 * shards, 1, lanes), jnp.float32),
                dma((6,)),
                dma((3,)),
                dma((3,)),
                dma((4, QUARTERS, 2)),
                dma((TEAM, QUARTERS, 2)),
                dma((2 * slots,)),
                dma((slots,)),
                dma((sections * shards,)),
                dma((2 * shards,)),
            ],
            compiler_params=pltpu.CompilerParams(
                collective_id=0,
                has_side_effects=True,
                vmem_limit_bytes=58 * 1024 * 1024,
            ),
        )(
            depths.T,
            widths.T,
            labels,
            patches,
            gains,
            token_first,
            token_second,
            channel_first,
            channel_second,
            final_gain[None, :],
            head_weight.T,
        )
        return line[0, :candidates]

    return jax.shard_map(
        local,
        mesh=mesh,
        in_specs=(
            P("ba", None, None),
            P("aa", None, None),
            P("aa", None, None),
            P("aa", None, None),
            P("aa", None, None),
            P("aa", None, None),
            P(),
            P(),
            P(),
            P(),
            P("ba"),
        ),
        out_specs=P(),
        check_vma=False,
    )
```

```python
import functools

import jax
import jax.numpy as jnp
from jax import lax
from jax.experimental import pallas as pl
from jax.experimental.pallas import tpu as pltpu
from jax.sharding import PartitionSpec as P

UNIT = 4
QUARTERS = 4
TEAM = 4
PARTS = 2
LAG = 2
DETOUR = 2
MESH = pl.DeviceIdType.MESH
GELU_A = 0.7978845608028654
GELU_B = 0.044715 * GELU_A


def layer_norm(values, gain):
    center = values - jnp.mean(values, axis=-1, keepdims=True)
    spread = jnp.mean(center * center, axis=-1, keepdims=True)
    return center * lax.rsqrt(spread + 1e-06) * gain


def quick_norm(values, gain, pivot=None):
    if pivot is not None:
        values = values - pivot
    mean = jnp.mean(values, axis=-1, keepdims=True)
    square = jnp.mean(values * values, axis=-1, keepdims=True)
    spread = jnp.maximum(square - mean * mean, 0.0)
    return (values - mean) * lax.rsqrt(spread + 1e-06) * gain, mean


def gelu(x, half):
    x = x.astype(jnp.bfloat16)
    bent = jnp.tanh(x * (jnp.bfloat16(GELU_A) + jnp.bfloat16(GELU_B) * (x * x)))
    scaled = x * half
    return scaled + scaled * bent


def dot(a, b):
    return jnp.dot(a, b, preferred_element_type=jnp.float32)


def token_mix(floats, gain, token_one_t, token_two, quick=False):
    model = floats[0].shape[1]
    if quick:
        pairs = [quick_norm(value, gain) for value in floats]
        normed = [norm for norm, _ in pairs]
        means = jnp.concatenate([mean for _, mean in pairs], axis=0)
    else:
        normed = [layer_norm(value, gain) for value in floats]
        means = None
    normed = jnp.concatenate([norm.astype(jnp.bfloat16) for norm in normed], axis=1)
    hidden = gelu(dot(token_one_t, normed), jnp.bfloat16(0.5))
    part = dot(token_two, hidden)
    mixed = jnp.concatenate(
        [
            value + part[:, unit * model : (unit + 1) * model]
            for unit, value in enumerate(floats)
        ],
        axis=0,
    )
    return (mixed, means) if quick else mixed


def kernel(
    sections,
    shards,
    depths,
    widths,
    labels,
    patches,
    gains,
    token_first,
    token_second,
    channel_first,
    channel_second,
    final_gain,
    head_weight_t,
    out,
    inbox,
    outbox,
    options,
    token_one,
    token_two,
    token_one_t,
    channel_one,
    channel_two,
    gain_pair,
    head,
    pooled,
    share,
    landing,
    stop_one,
    stop_two,
    load_sem,
    small_send,
    small_recv,
    weight_send,
    weight_recv,
    stop_send,
    stop_recv,
    state_send,
    state_recv,
    share_send,
    landing_sem,
):
    section = lax.axis_index("aa")
    shard = lax.axis_index("ba")
    pair = section // 2
    side = section % 2
    pairs = sections // 2
    last = pairs - 1
    images, patch_count, model = patches.shape
    candidates = depths.shape[1]
    per = candidates // 2
    slots = per * images
    hidden_units = channel_first.shape[2]
    quarter = hidden_units // QUARTERS
    partner = section + 1 - 2 * side
    rank = shard % TEAM
    team = shard - rank
    beside = team + rank + 1 - 2 * (rank % 2)
    across = team + (rank + 2) % TEAM

    loads = [
        pltpu.make_async_copy(source.at[0], target.at[side], load_sem.at[index])
        for index, (source, target) in enumerate(
            (
                (token_first, token_one),
                (token_second, token_two),
                (channel_first, channel_one),
                (channel_second, channel_two),
                (gains, gain_pair),
            )
        )
    ]
    head_load = pltpu.make_async_copy(head_weight_t, head, load_sem.at[5])
    for load in loads:
        load.start()

    @pl.when(pair == last)
    def _():
        head_load.start()

    barrier = pltpu.get_barrier_semaphore()

    def greet(aa, ba):
        pl.semaphore_signal(barrier, inc=1, device_id=(aa, ba), device_id_type=MESH)

    @pl.when(pair == 0)
    def _():
        greet(partner, shard)

    @pl.when(pair == 1)
    def _():
        greet(side, shard)

    @pl.when(pair > 0)
    def _():
        greet(partner, shard)
        greet(section, beside)
        greet(section, across)

    @pl.when(pair > 1)
    def _():
        greet(section - 2, shard)
        greet(partner - 2, shard)

    @pl.when(jnp.logical_and(pair > 0, pair < last))
    def _():
        greet(section + 2, shard)

    def greet_last(target, carry):
        aa, ba = 2 * last + target // shards, target % shards

        @pl.when(jnp.logical_or(aa != section, ba != shard))
        def _():
            greet(aa, ba)

        return carry

    lax.fori_loop(0, 2 * shards, greet_last, 0)

    @pl.when(section == 1)
    def _():
        pl.semaphore_wait(barrier, 2)

    @pl.when(jnp.logical_and(pair == 1, pair < last))
    def _():
        pl.semaphore_wait(barrier, 5)

    @pl.when(jnp.logical_and(pair > 1, pair < last))
    def _():
        pl.semaphore_wait(barrier, 6)

    @pl.when(pair == last)
    def _():
        pl.semaphore_wait(barrier, sections * shards + (3 if last > 1 else 2))

    def state_copy(source, target, aa):
        return pltpu.make_async_remote_copy(
            src_ref=outbox.at[source],
            dst_ref=inbox.at[target],
            send_sem=state_send.at[source],
            recv_sem=state_recv.at[target],
            device_id=(aa, shard),
            device_id_type=MESH,
        )

    def arrived(slot):
        state_copy(slot, slot, section).wait_recv()

    @pl.when(section == 0)
    def _():
        for load in loads:
            load.wait()
        floats = [patches[image].astype(jnp.float32) for image in range(images)]
        mixed = token_mix(floats, gain_pair[0, 0:1, :], token_one[0].T, token_two[0])
        second = layer_norm(mixed, gain_pair[0, 1:2, :]).astype(jnp.bfloat16)
        total = mixed
        for width in range(QUARTERS):
            cut = slice(width * quarter, (width + 1) * quarter)
            hidden = gelu(dot(second, channel_one[0, :, cut]), jnp.bfloat16(0.5))
            total = total + dot(hidden, channel_two[0, cut, :])
            rounded = total.astype(jnp.bfloat16)
            for image in range(images):
                slot = image * QUARTERS + width
                outbox[slot] = rounded[image * patch_count : (image + 1) * patch_count]
        pl.semaphore_wait(barrier, 2)
        for slot in range(images * QUARTERS):
            state_copy(slot, slot, 1).start()

        def relay(slot):
            return pltpu.make_async_remote_copy(
                src_ref=inbox.at[slot],
                dst_ref=inbox.at[slot],
                send_sem=state_send.at[slots + slot],
                recv_sem=state_recv.at[slot],
                device_id=(2, shard),
                device_id_type=MESH,
            )

        def pass_on(slot, carry):
            arrived(slot)
            relay(slot).start()
            return carry

        def drain(slot, carry):
            relay(slot).wait_send()
            return carry

        lax.fori_loop(0, slots, pass_on, 0)
        lax.fori_loop(0, slots, drain, 0)
        for slot in range(images * QUARTERS):
            state_copy(slot, slot, 1).wait_send()

    @pl.when(section == 1)
    def _():
        for load in loads:
            load.wait()

        def image_step(image, carry):
            base = image * QUARTERS
            for width in range(QUARTERS):
                arrived(base + width)
            states = [inbox[base + width] for width in range(QUARTERS)]
            floats = [state.astype(jnp.float32) for state in states]
            mixed = token_mix(
                floats, gain_pair[1, 0:1, :], token_one[1].T, token_two[1]
            )
            second = layer_norm(mixed, gain_pair[1, 1:2, :]).astype(jnp.bfloat16)
            total = mixed
            for first in range(QUARTERS):
                options[first] = states[first]
            for width in range(QUARTERS):
                cut = slice(width * quarter, (width + 1) * quarter)
                hidden = gelu(dot(second, channel_one[1, :, cut]), jnp.bfloat16(0.5))
                total = total + dot(hidden, channel_two[1, cut, :])
                rounded = total.astype(jnp.bfloat16)
                for first in range(QUARTERS):
                    options[(width + 1) * QUARTERS + first] = rounded[
                        first * patch_count : (first + 1) * patch_count
                    ]

            def pick(index, carry):
                for parity in range(2):
                    candidate = 2 * index + parity
                    active = 1 < depths[0, candidate]
                    chosen = jnp.where(active, widths[1, candidate], 0)
                    row = chosen * QUARTERS + jnp.maximum(widths[0, candidate], 1) - 1
                    slot = image * per + index
                    outbox[parity * slots + slot] = options[row]
                    state_copy(parity * slots + slot, slot, 3 * parity).start()
                return carry

            lax.fori_loop(0, per, pick, 0)
            return carry

        lax.fori_loop(0, images, image_step, 0)

        def drain(index, carry):
            state_copy(index, index % slots, 2).wait_send()
            return carry

        lax.fori_loop(0, 2 * slots, drain, 0)

    rounds = QUARTERS
    piece = quarter // TEAM

    def region(turn, owner, part):
        start = turn * quarter + owner * piece
        rows, thin = model // PARTS, piece // PARTS
        return (
            (
                pl.ds(part * rows, rows),
                pl.ds(pl.multiple_of(start, piece), piece),
            ),
            (
                pl.ds(pl.multiple_of(start + part * thin, thin), thin),
                slice(None),
            ),
        )

    def weight_copy(parity, from_input, kind, turn, part, owner, aa, ba, which):
        rows, columns = region(turn, owner, part)[which]
        target = (channel_one, channel_two)[which].at[parity, rows, columns]
        if from_input:
            ref = (channel_first, channel_second)[which].at[0, rows, columns]
        else:
            ref = target
        return pltpu.make_async_remote_copy(
            src_ref=ref,
            dst_ref=target,
            send_sem=weight_send.at[kind, turn, part, which],
            recv_sem=weight_recv.at[owner, turn, part, which],
            device_id=(aa, ba),
            device_id_type=MESH,
        )

    other = 1 - side

    def small_copies(part):
        return [
            pltpu.make_async_remote_copy(
                src_ref=source.at[0],
                dst_ref=target.at[part],
                send_sem=small_send.at[index],
                recv_sem=small_recv.at[index],
                device_id=(partner, shard),
                device_id_type=MESH,
            )
            for index, (source, target) in enumerate(
                (
                    (token_first, token_one),
                    (token_second, token_two),
                    (gains, gain_pair),
                )
            )
        ]

    rank_beside = rank + 1 - 2 * (rank % 2)
    rank_across = (rank + 2) % TEAM
    rank_far = (rank_beside + 2) % TEAM

    def to_partner(turn, part, which):
        return weight_copy(side, True, 0, turn, part, rank, partner, shard, which)

    def to_across(turn, part, which):
        return weight_copy(other, False, 1, turn, part, rank, section, across, which)

    def to_beside(turn, part, which):
        return weight_copy(other, False, 2, turn, part, rank, section, beside, which)

    def to_beside_again(turn, part, which):
        return weight_copy(
            other, False, 3, turn, part, rank_across, section, beside, which
        )

    def from_owner(turn, owner, part, which):
        return weight_copy(other, False, 0, turn, part, owner, section, shard, which)

    def stop(part, which):
        if which == 0:
            rows = model // PARTS
            return stop_one.at[pl.ds(part * rows, rows), :]
        thin = piece // PARTS
        return stop_two.at[pl.ds(part * thin, thin), :]

    def detour(part, which):
        rows, columns = region(DETOUR, rank, part)[which]
        return pltpu.make_async_remote_copy(
            src_ref=(channel_first, channel_second)[which].at[0, rows, columns],
            dst_ref=stop(part, which),
            send_sem=weight_send.at[0, DETOUR, part, which],
            recv_sem=stop_recv.at[part, which],
            device_id=(lax.rem(partner + 2, sections), shard),
            device_id_type=MESH,
        )

    def pass_down(part, which):
        rows, columns = region(DETOUR, rank, part)[which]
        return pltpu.make_async_remote_copy(
            src_ref=stop(part, which),
            dst_ref=(channel_one, channel_two)[which].at[other, rows, columns],
            send_sem=stop_send.at[part, which],
            recv_sem=weight_recv.at[rank, DETOUR, part, which],
            device_id=(lax.rem(section + sections - 2, sections), shard),
            device_id_type=MESH,
        )

    def for_parts(act):
        def visit(index, carry):
            for which in range(2):
                act(index // PARTS, index % PARTS, which)
            return carry

        lax.fori_loop(0, rounds * PARTS, visit, 0)

    def section_step(group, first, finish, parity, states):
        here = 2 * pair + parity
        floats = [state.astype(jnp.float32) for state in states]
        mixed, means = token_mix(
            floats,
            gain_pair[parity, 0:1, :],
            token_one_t[parity],
            token_two[parity],
            quick=True,
        )
        second, _ = quick_norm(mixed, gain_pair[parity, 1:2, :], means)
        second = second.astype(jnp.bfloat16)
        pre = dot(second, channel_one[parity])
        lane = lax.broadcasted_iota(jnp.int32, (1, hidden_units), 1)
        parts = []
        actives = []
        for unit in range(group):
            candidate = 2 * ((first + unit) % per) + side
            actives.append(here % UNIT < depths[here // UNIT, candidate])
            half = jnp.where(lane < widths[here, candidate] * quarter, 0.5, 0.0).astype(
                jnp.bfloat16
            )
            rows = slice(unit * patch_count, (unit + 1) * patch_count)
            parts.append(gelu(pre[rows], half))
        hidden = jnp.concatenate(parts, axis=0)
        total = (mixed + dot(hidden, channel_two[parity])).astype(jnp.bfloat16)
        return [
            jnp.where(
                actives[unit],
                total[unit * patch_count : (unit + 1) * patch_count],
                states[unit],
            )
            for unit in range(group)
        ]

    def chunk(group, offset, index, carry):
        first = offset + index * group
        for unit in range(group):
            arrived(first + unit)

        def both(parity, carry):
            states = [inbox[first + unit] for unit in range(group)]
            updated = section_step(group, first, False, parity, states)
            for unit in range(group):
                outbox[first + unit] = updated[unit]

            @pl.when(parity == 0)
            def _():
                for unit in range(group):
                    inbox[first + unit] = updated[unit]

            return carry

        lax.fori_loop(0, 2, both, 0)

        @pl.when(pair < last)
        def _():
            for unit in range(group):
                state_copy(first + unit, first + unit, section + 2).start()

        @pl.when(pair == last)
        def _():
            for unit in range(group):
                final = layer_norm(
                    outbox[first + unit].astype(jnp.float32), final_gain[...]
                )
                pooled[pl.ds(first + unit, 1), :] = jnp.mean(
                    final, axis=0, keepdims=True
                )

        return carry

    @pl.when(pair > 0)
    def _():
        for copy in small_copies(side):
            copy.start()
        def send(turn, part, which):
            around = jnp.logical_and(turn == DETOUR, pair < last)

            @pl.when(around)
            def _():
                detour(part, which).start()

            @pl.when(jnp.logical_not(around))
            def _():
                to_partner(turn, part, which).start()

        for_parts(send)
        for load in loads:
            load.wait()
        token_one_t[side] = token_one[side].T
        for copy in small_copies(other):
            copy.wait_recv()
        token_one_t[other] = token_one[other].T
        def forward(turn, part, which):
            @pl.when(jnp.logical_and(turn == 0, pair > 1))
            def _():
                detour(part, which).wait_recv()
                pass_down(part, which).start()

            from_owner(turn, rank, part, which).wait_recv()
            to_across(turn, part, which).start()
            to_beside(turn, part, which).start()
            before = turn * PARTS + part - LAG
            if which == 1:

                @pl.when(before >= 0)
                def _():
                    forward_again(before)

        def forward_again(index):
            turn, part = index // PARTS, index % PARTS
            for which in range(2):
                from_owner(turn, rank_across, part, which).wait_recv()
                to_beside_again(turn, part, which).start()

        def finish(turn, part, which):
            from_owner(turn, rank_beside, part, which).wait_recv()
            from_owner(turn, rank_far, part, which).wait_recv()

        for_parts(forward)
        for index in range(rounds * PARTS - LAG, rounds * PARTS):
            forward_again(index)
        for_parts(finish)
        group = 2 if slots % 2 == 0 else 1
        lax.fori_loop(0, slots // group, functools.partial(chunk, group, 0), 0)
        for copy in small_copies(side):
            copy.wait_send()
        def settle(turn, part, which):
            for copy in (to_partner, to_across, to_beside, to_beside_again):
                copy(turn, part, which).wait_send()

            @pl.when(jnp.logical_and(turn == 0, pair > 1))
            def _():
                pass_down(part, which).wait_send()

        for_parts(settle)

    @pl.when(jnp.logical_and(pair > 0, pair < last))
    def _():
        def drain(slot, carry):
            state_copy(slot, slot, section + 2).wait_send()
            return carry

        lax.fori_loop(0, slots, drain, 0)

    def tell(aa, ba):
        mine = side * shards + shard
        return pltpu.make_async_remote_copy(
            src_ref=share,
            dst_ref=landing.at[mine],
            send_sem=share_send.at[aa * shards + ba],
            recv_sem=landing_sem.at[mine],
            device_id=(aa, ba),
            device_id_type=MESH,
        )

    def each_other(act):
        def visit(target, carry):
            aa, ba = target // shards, target % shards

            @pl.when(jnp.logical_or(aa != section, ba != shard))
            def _():
                act(tell(aa, ba))

            return carry

        lax.fori_loop(0, sections * shards, visit, 0)

    def heard(aa, ba, origin):
        pltpu.make_async_remote_copy(
            src_ref=share,
            dst_ref=landing.at[origin],
            send_sem=share_send.at[0],
            recv_sem=landing_sem.at[origin],
            device_id=(aa, ba),
            device_id_type=MESH,
        ).wait_recv()

    @pl.when(pair == last)
    def _():
        head_load.wait()
        logits = lax.dot_general(
            pooled[...].astype(jnp.bfloat16),
            head[...],
            (((1,), (1,)), ((), ())),
            preferred_element_type=jnp.float32,
        )
        top = jnp.max(logits, axis=-1, keepdims=True)
        total = top + jnp.log(jnp.sum(jnp.exp(logits - top), axis=-1, keepdims=True))
        rows = lax.broadcasted_iota(jnp.int32, logits.shape, 0)
        classes = lax.broadcasted_iota(jnp.int32, logits.shape, 1)
        wanted = jnp.full(logits.shape, labels[0], jnp.int32)
        for image in range(1, images):
            wanted = jnp.where(rows >= image * per, labels[image], wanted)
        picked = jnp.sum(
            jnp.where(classes == wanted, logits, 0.0), axis=-1, keepdims=True
        )
        losses = total - picked
        summed = losses[:per]
        for image in range(1, images):
            summed = summed + losses[image * per : (image + 1) * per]
        lanes = out.shape[1]
        rows = lax.broadcasted_iota(jnp.int32, (per, lanes), 0)
        cols = lax.broadcasted_iota(jnp.int32, (per, lanes), 1)
        spread = jnp.broadcast_to(summed, (per, lanes))
        line = jnp.sum(
            jnp.where(2 * rows + side == cols, spread, 0.0), axis=0, keepdims=True
        )
        share[...] = line
        landing[side * shards + shard] = line
        each_other(lambda copy: copy.start())
        each_other(lambda copy: copy.wait_send())

    for origin in range(2 * shards):
        aa, ba = 2 * last + origin // shards, origin % shards

        @pl.when(jnp.logical_or(section != aa, shard != ba))
        def _():
            heard(aa, ba, origin)

    result = landing[0]
    for origin in range(1, 2 * shards):
        result = result + landing[origin]
    out[...] = result


def solution(mesh):
    sections, shards = mesh.shape["aa"], mesh.shape["ba"]

    def local(
        patches,
        token_first,
        token_second,
        channel_first,
        channel_second,
        gains,
        final_gain,
        head_weight,
        depths,
        widths,
        labels,
    ):
        images, patch_count, model = patches.shape
        candidates = depths.shape[0]
        slots = candidates // 2 * images
        piece = channel_first.shape[2] // (QUARTERS * TEAM)
        lanes = pl.cdiv(candidates, 128) * 128
        smem = pl.BlockSpec(memory_space=pltpu.SMEM)
        vmem = pl.BlockSpec(memory_space=pltpu.VMEM)
        hbm = pl.BlockSpec(memory_space=pltpu.HBM)
        bf16 = jnp.bfloat16
        dma = pltpu.SemaphoreType.DMA
        line = pl.pallas_call(
            functools.partial(kernel, sections, shards),
            out_shape=jax.ShapeDtypeStruct((1, lanes), jnp.float32),
            in_specs=[smem] * 3 + [vmem] + [hbm] * 5 + [vmem] + [hbm],
            out_specs=vmem,
            scratch_shapes=[
                pltpu.VMEM((slots, patch_count, model), bf16),
                pltpu.VMEM((2 * slots, patch_count, model), bf16),
                pltpu.VMEM(((QUARTERS + 1) * QUARTERS, patch_count, model), bf16),
                pltpu.VMEM((2,) + token_first.shape[1:], bf16),
                pltpu.VMEM((2,) + token_second.shape[1:], bf16),
                pltpu.VMEM((2, token_first.shape[2], patch_count), bf16),
                pltpu.VMEM((2,) + channel_first.shape[1:], bf16),
                pltpu.VMEM((2,) + channel_second.shape[1:], bf16),
                pltpu.VMEM((2,) + gains.shape[1:], jnp.float32),
                pltpu.VMEM(head_weight.shape[::-1], bf16),
                pltpu.VMEM((slots, model), jnp.float32),
                pltpu.VMEM((1, lanes), jnp.float32),
                pltpu.VMEM((2 * shards, 1, lanes), jnp.float32),
                pltpu.VMEM((model, piece), bf16),
                pltpu.VMEM((piece, model), bf16),
                dma((6,)),
                dma((3,)),
                dma((3,)),
                dma((4, QUARTERS, PARTS, 2)),
                dma((TEAM, QUARTERS, PARTS, 2)),
                dma((PARTS, 2)),
                dma((PARTS, 2)),
                dma((2 * slots,)),
                dma((slots,)),
                dma((sections * shards,)),
                dma((2 * shards,)),
            ],
            compiler_params=pltpu.CompilerParams(
                collective_id=0,
                has_side_effects=True,
                vmem_limit_bytes=58 * 1024 * 1024,
            ),
        )(
            depths.T,
            widths.T,
            labels,
            patches,
            gains,
            token_first,
            token_second,
            channel_first,
            channel_second,
            final_gain[None, :],
            head_weight.T,
        )
        return line[0, :candidates]

    return jax.shard_map(
        local,
        mesh=mesh,
        in_specs=(
            P("ba", None, None),
            P("aa", None, None),
            P("aa", None, None),
            P("aa", None, None),
            P("aa", None, None),
            P("aa", None, None),
            P(),
            P(),
            P(),
            P(),
            P("ba"),
        ),
        out_specs=P(),
        check_vma=False,
    )
```

```python
import functools

import jax
import jax.numpy as jnp
from jax import lax
from jax.experimental import pallas as pl
from jax.experimental.pallas import tpu as pltpu
from jax.sharding import PartitionSpec as P

UNIT = 4
QUARTERS = 4
TEAM = 4
PARTS = 2
LAG = 2
AHEAD = 2
MESH = pl.DeviceIdType.MESH
GELU_A = 0.7978845608028654
GELU_B = 0.044715 * GELU_A


def layer_norm(values, gain):
    center = values - jnp.mean(values, axis=-1, keepdims=True)
    spread = jnp.mean(center * center, axis=-1, keepdims=True)
    return center * lax.rsqrt(spread + 1e-06) * gain


def quick_norm(values, gain, pivot=None):
    if pivot is not None:
        values = values - pivot
    mean = jnp.mean(values, axis=-1, keepdims=True)
    square = jnp.mean(values * values, axis=-1, keepdims=True)
    spread = jnp.maximum(square - mean * mean, 0.0)
    return (values - mean) * lax.rsqrt(spread + 1e-06) * gain, mean


def gelu(x, half):
    x = x.astype(jnp.bfloat16)
    bent = jnp.tanh(x * (jnp.bfloat16(GELU_A) + jnp.bfloat16(GELU_B) * (x * x)))
    scaled = x * half
    return scaled + scaled * bent


def dot(a, b):
    return jnp.dot(a, b, preferred_element_type=jnp.float32)


def token_mix(floats, gain, token_one_t, token_two, quick=False):
    model = floats[0].shape[1]
    if quick:
        pairs = [quick_norm(value, gain) for value in floats]
        normed = [norm for norm, _ in pairs]
        means = jnp.concatenate([mean for _, mean in pairs], axis=0)
    else:
        normed = [layer_norm(value, gain) for value in floats]
        means = None
    normed = jnp.concatenate([norm.astype(jnp.bfloat16) for norm in normed], axis=1)
    hidden = gelu(dot(token_one_t, normed), jnp.bfloat16(0.5))
    part = dot(token_two, hidden)
    mixed = jnp.concatenate(
        [
            value + part[:, unit * model : (unit + 1) * model]
            for unit, value in enumerate(floats)
        ],
        axis=0,
    )
    return (mixed, means) if quick else mixed


def kernel(
    sections,
    shards,
    depths_in,
    widths_in,
    labels_in,
    patches_in,
    gains,
    token_first,
    token_second,
    channel_first,
    channel_second,
    final_gain_in,
    head_weight_t,
    out,
    depths,
    widths,
    labels,
    patches,
    final_gain,
    inbox,
    outbox,
    options,
    token_one,
    token_two,
    token_one_t,
    channel_one,
    channel_two,
    gain_pair,
    head,
    pooled,
    share,
    landing,
    load_sem,
    small_send,
    small_recv,
    weight_send,
    weight_recv,
    state_send,
    state_recv,
    share_send,
    landing_sem,
):
    section = lax.axis_index("aa")
    shard = lax.axis_index("ba")
    pair = section // 2
    side = section % 2
    pairs = sections // 2
    last = pairs - 1
    images, patch_count, model = patches_in.shape
    candidates = depths_in.shape[1]
    per = candidates // 2
    slots = per * images
    hidden_units = channel_first.shape[2]
    quarter = hidden_units // QUARTERS
    partner = section + 1 - 2 * side
    rank = shard % TEAM
    team = shard - rank
    beside = team + rank + 1 - 2 * (rank % 2)
    across = team + (rank + 2) % TEAM

    loads = [
        pltpu.make_async_copy(source.at[0], target.at[side], load_sem.at[index])
        for index, (source, target) in enumerate(
            (
                (token_first, token_one),
                (token_second, token_two),
                (channel_first, channel_one),
                (channel_second, channel_two),
                (gains, gain_pair),
            )
        )
    ]
    head_load = pltpu.make_async_copy(head_weight_t, head, load_sem.at[5])
    tables = [
        pltpu.make_async_copy(source, target, load_sem.at[6 + index])
        for index, (source, target) in enumerate(
            (
                (patches_in, patches),
                (depths_in, depths),
                (widths_in, widths),
                (labels_in, labels),
                (final_gain_in, final_gain),
            )
        )
    ]
    loads = loads + tables
    for load in loads:
        load.start()

    @pl.when(pair == last)
    def _():
        head_load.start()

    barrier = pltpu.get_barrier_semaphore()

    def greet(aa, ba):
        pl.semaphore_signal(barrier, inc=1, device_id=(aa, ba), device_id_type=MESH)

    @pl.when(pair == 0)
    def _():
        greet(partner, shard)

    @pl.when(pair == 1)
    def _():
        greet(side, shard)

    @pl.when(pair > 0)
    def _():
        greet(partner, shard)
        greet(section, beside)
        greet(section, across)

    @pl.when(pair > 1)
    def _():
        greet(section - 2, shard)

    def greet_last(target, carry):
        aa, ba = 2 * last + target // shards, target % shards

        @pl.when(jnp.logical_or(aa != section, ba != shard))
        def _():
            greet(aa, ba)

        return carry

    lax.fori_loop(0, 2 * shards, greet_last, 0)

    @pl.when(section == 1)
    def _():
        pl.semaphore_wait(barrier, 2)

    @pl.when(jnp.logical_and(pair > 0, pair < last))
    def _():
        pl.semaphore_wait(barrier, 4)

    @pl.when(pair == last)
    def _():
        pl.semaphore_wait(barrier, sections * shards + 2)

    def state_copy(source, target, aa):
        return pltpu.make_async_remote_copy(
            src_ref=outbox.at[source],
            dst_ref=inbox.at[target],
            send_sem=state_send.at[source],
            recv_sem=state_recv.at[target],
            device_id=(aa, shard),
            device_id_type=MESH,
        )

    def arrived(slot):
        state_copy(slot, slot, section).wait_recv()

    @pl.when(section == 0)
    def _():
        for load in loads:
            load.wait()
        floats = [patches[image].astype(jnp.float32) for image in range(images)]
        mixed = token_mix(floats, gain_pair[0, 0:1, :], token_one[0].T, token_two[0])
        second = layer_norm(mixed, gain_pair[0, 1:2, :]).astype(jnp.bfloat16)
        total = mixed
        for width in range(QUARTERS):
            cut = slice(width * quarter, (width + 1) * quarter)
            hidden = gelu(dot(second, channel_one[0, :, cut]), jnp.bfloat16(0.5))
            total = total + dot(hidden, channel_two[0, cut, :])
            rounded = total.astype(jnp.bfloat16)
            for image in range(images):
                slot = image * QUARTERS + width
                outbox[slot] = rounded[image * patch_count : (image + 1) * patch_count]
        pl.semaphore_wait(barrier, 2)
        for slot in range(images * QUARTERS):
            state_copy(slot, slot, 1).start()

        def relay(slot):
            return pltpu.make_async_remote_copy(
                src_ref=inbox.at[slot],
                dst_ref=inbox.at[slot],
                send_sem=state_send.at[slots + slot],
                recv_sem=state_recv.at[slot],
                device_id=(2, shard),
                device_id_type=MESH,
            )

        def pass_on(slot, carry):
            arrived(slot)
            relay(slot).start()
            return carry

        def drain(slot, carry):
            relay(slot).wait_send()
            return carry

        lax.fori_loop(0, slots, pass_on, 0)
        lax.fori_loop(0, slots, drain, 0)
        for slot in range(images * QUARTERS):
            state_copy(slot, slot, 1).wait_send()

    @pl.when(section == 1)
    def _():
        for load in loads:
            load.wait()

        def image_step(image, carry):
            base = image * QUARTERS
            for width in range(QUARTERS):
                arrived(base + width)
            states = [inbox[base + width] for width in range(QUARTERS)]
            floats = [state.astype(jnp.float32) for state in states]
            mixed = token_mix(
                floats, gain_pair[1, 0:1, :], token_one[1].T, token_two[1]
            )
            second = layer_norm(mixed, gain_pair[1, 1:2, :]).astype(jnp.bfloat16)
            total = mixed
            for first in range(QUARTERS):
                options[first] = states[first]
            for width in range(QUARTERS):
                cut = slice(width * quarter, (width + 1) * quarter)
                hidden = gelu(dot(second, channel_one[1, :, cut]), jnp.bfloat16(0.5))
                total = total + dot(hidden, channel_two[1, cut, :])
                rounded = total.astype(jnp.bfloat16)
                for first in range(QUARTERS):
                    options[(width + 1) * QUARTERS + first] = rounded[
                        first * patch_count : (first + 1) * patch_count
                    ]

            def pick(index, carry):
                for parity in range(2):
                    candidate = 2 * index + parity
                    active = 1 < depths[0, candidate]
                    chosen = jnp.where(active, widths[1, candidate], 0)
                    row = chosen * QUARTERS + jnp.maximum(widths[0, candidate], 1) - 1
                    slot = image * per + index
                    outbox[parity * slots + slot] = options[row]
                    state_copy(parity * slots + slot, slot, 3 * parity).start()
                return carry

            lax.fori_loop(0, per, pick, 0)
            return carry

        lax.fori_loop(0, images, image_step, 0)

        def drain(index, carry):
            state_copy(index, index % slots, 2).wait_send()
            return carry

        lax.fori_loop(0, 2 * slots, drain, 0)

    rounds = QUARTERS

    def region(turn, owner, part):
        spans = []
        for height in (model, hidden_units):
            rows = height // (rounds * TEAM * PARTS)
            start = ((turn * TEAM + owner) * PARTS + part) * rows
            spans.append((pl.ds(pl.multiple_of(start, rows), rows), slice(None)))
        return spans

    def weight_copy(parity, from_input, kind, turn, part, owner, aa, ba, which):
        rows, columns = region(turn, owner, part)[which]
        target = (channel_one, channel_two)[which].at[parity, rows, columns]
        if from_input:
            ref = (channel_first, channel_second)[which].at[0, rows, columns]
        else:
            ref = target
        return pltpu.make_async_remote_copy(
            src_ref=ref,
            dst_ref=target,
            send_sem=weight_send.at[kind, turn, part, which],
            recv_sem=weight_recv.at[owner, turn, part, which],
            device_id=(aa, ba),
            device_id_type=MESH,
        )

    other = 1 - side

    def small_copies(part):
        return [
            pltpu.make_async_remote_copy(
                src_ref=source.at[0],
                dst_ref=target.at[part],
                send_sem=small_send.at[index],
                recv_sem=small_recv.at[index],
                device_id=(partner, shard),
                device_id_type=MESH,
            )
            for index, (source, target) in enumerate(
                (
                    (token_first, token_one),
                    (token_second, token_two),
                    (gains, gain_pair),
                )
            )
        ]

    rank_beside = rank + 1 - 2 * (rank % 2)
    rank_across = (rank + 2) % TEAM
    rank_far = (rank_beside + 2) % TEAM

    def to_partner(turn, part, which):
        return weight_copy(side, True, 0, turn, part, rank, partner, shard, which)

    def to_across(turn, part, which):
        return weight_copy(other, False, 1, turn, part, rank, section, across, which)

    def to_beside(turn, part, which):
        return weight_copy(other, False, 2, turn, part, rank, section, beside, which)

    def to_beside_again(turn, part, which):
        return weight_copy(
            other, False, 3, turn, part, rank_across, section, beside, which
        )

    def from_owner(turn, owner, part, which):
        return weight_copy(other, False, 0, turn, part, owner, section, shard, which)

    def for_parts(act):
        def visit(index, carry):
            for which in range(2):
                act(index // PARTS, index % PARTS, which)
            return carry

        lax.fori_loop(0, rounds * PARTS, visit, 0)

    def section_step(group, first, finish, parity, states):
        here = 2 * pair + parity
        floats = [state.astype(jnp.float32) for state in states]
        mixed, means = token_mix(
            floats,
            gain_pair[parity, 0:1, :],
            token_one_t[parity],
            token_two[parity],
            quick=True,
        )
        second, _ = quick_norm(mixed, gain_pair[parity, 1:2, :], means)
        second = second.astype(jnp.bfloat16)
        pre = dot(second, channel_one[parity])
        lane = lax.broadcasted_iota(jnp.int32, (1, hidden_units), 1)
        parts = []
        actives = []
        for unit in range(group):
            candidate = 2 * ((first + unit) % per) + side
            actives.append(here % UNIT < depths[here // UNIT, candidate])
            half = jnp.where(lane < widths[here, candidate] * quarter, 0.5, 0.0).astype(
                jnp.bfloat16
            )
            rows = slice(unit * patch_count, (unit + 1) * patch_count)
            parts.append(gelu(pre[rows], half))
        hidden = jnp.concatenate(parts, axis=0)
        total = (mixed + dot(hidden, channel_two[parity])).astype(jnp.bfloat16)
        return [
            jnp.where(
                actives[unit],
                total[unit * patch_count : (unit + 1) * patch_count],
                states[unit],
            )
            for unit in range(group)
        ]

    def chunk(group, offset, index, carry):
        first = offset + index * group
        for unit in range(group):
            arrived(first + unit)

        def both(parity, carry):
            states = [inbox[first + unit] for unit in range(group)]
            updated = section_step(group, first, False, parity, states)
            for unit in range(group):
                outbox[first + unit] = updated[unit]

            @pl.when(parity == 0)
            def _():
                for unit in range(group):
                    inbox[first + unit] = updated[unit]

            return carry

        lax.fori_loop(0, 2, both, 0)

        @pl.when(pair < last)
        def _():
            for unit in range(group):
                state_copy(first + unit, first + unit, section + 2).start()

        @pl.when(pair == last)
        def _():
            for unit in range(group):
                final = layer_norm(
                    outbox[first + unit].astype(jnp.float32), final_gain[...]
                )
                pooled[pl.ds(first + unit, 1), :] = jnp.mean(
                    final, axis=0, keepdims=True
                )

        return carry

    @pl.when(pair > 0)
    def _():
        for copy in small_copies(side):
            copy.start()
        for index in range(AHEAD):
            for which in range(2):
                to_partner(index // PARTS, index % PARTS, which).start()

        for load in loads:
            load.wait()
        token_one_t[side] = token_one[side].T
        for copy in small_copies(other):
            copy.wait_recv()
        token_one_t[other] = token_one[other].T
        def forward(turn, part, which):
            from_owner(turn, rank, part, which).wait_recv()
            to_across(turn, part, which).start()
            to_beside(turn, part, which).start()
            follow = turn * PARTS + part + AHEAD

            @pl.when(follow < rounds * PARTS)
            def _():
                to_partner(follow // PARTS, follow % PARTS, which).start()

            before = turn * PARTS + part - LAG
            if which == 1:

                @pl.when(before >= 0)
                def _():
                    forward_again(before)

        def forward_again(index):
            turn, part = index // PARTS, index % PARTS
            for which in range(2):
                from_owner(turn, rank_across, part, which).wait_recv()
                to_beside_again(turn, part, which).start()

        def finish(turn, part, which):
            from_owner(turn, rank_beside, part, which).wait_recv()
            from_owner(turn, rank_far, part, which).wait_recv()

        for_parts(forward)
        for index in range(rounds * PARTS - LAG, rounds * PARTS):
            forward_again(index)
        for_parts(finish)
        group = 2 if slots % 2 == 0 else 1
        lax.fori_loop(0, slots // group, functools.partial(chunk, group, 0), 0)
        for copy in small_copies(side):
            copy.wait_send()
        def settle(turn, part, which):
            for copy in (to_partner, to_across, to_beside, to_beside_again):
                copy(turn, part, which).wait_send()

        for_parts(settle)

    @pl.when(jnp.logical_and(pair > 0, pair < last))
    def _():
        def drain(slot, carry):
            state_copy(slot, slot, section + 2).wait_send()
            return carry

        lax.fori_loop(0, slots, drain, 0)

    def tell(aa, ba):
        mine = side * shards + shard
        return pltpu.make_async_remote_copy(
            src_ref=share,
            dst_ref=landing.at[mine],
            send_sem=share_send.at[aa * shards + ba],
            recv_sem=landing_sem.at[mine],
            device_id=(aa, ba),
            device_id_type=MESH,
        )

    def each_other(act):
        def visit(target, carry):
            aa, ba = target // shards, target % shards

            @pl.when(jnp.logical_or(aa != section, ba != shard))
            def _():
                act(tell(aa, ba))

            return carry

        lax.fori_loop(0, sections * shards, visit, 0)

    def heard(aa, ba, origin):
        pltpu.make_async_remote_copy(
            src_ref=share,
            dst_ref=landing.at[origin],
            send_sem=share_send.at[0],
            recv_sem=landing_sem.at[origin],
            device_id=(aa, ba),
            device_id_type=MESH,
        ).wait_recv()

    @pl.when(pair == last)
    def _():
        head_load.wait()
        logits = lax.dot_general(
            pooled[...].astype(jnp.bfloat16),
            head[...],
            (((1,), (1,)), ((), ())),
            preferred_element_type=jnp.float32,
        )
        top = jnp.max(logits, axis=-1, keepdims=True)
        total = top + jnp.log(jnp.sum(jnp.exp(logits - top), axis=-1, keepdims=True))
        rows = lax.broadcasted_iota(jnp.int32, logits.shape, 0)
        classes = lax.broadcasted_iota(jnp.int32, logits.shape, 1)
        wanted = jnp.full(logits.shape, labels[0], jnp.int32)
        for image in range(1, images):
            wanted = jnp.where(rows >= image * per, labels[image], wanted)
        picked = jnp.sum(
            jnp.where(classes == wanted, logits, 0.0), axis=-1, keepdims=True
        )
        losses = total - picked
        summed = losses[:per]
        for image in range(1, images):
            summed = summed + losses[image * per : (image + 1) * per]
        lanes = out.shape[1]
        rows = lax.broadcasted_iota(jnp.int32, (per, lanes), 0)
        cols = lax.broadcasted_iota(jnp.int32, (per, lanes), 1)
        spread = jnp.broadcast_to(summed, (per, lanes))
        line = jnp.sum(
            jnp.where(2 * rows + side == cols, spread, 0.0), axis=0, keepdims=True
        )
        share[...] = line
        landing[side * shards + shard] = line
        each_other(lambda copy: copy.start())
        each_other(lambda copy: copy.wait_send())

    for origin in range(2 * shards):
        aa, ba = 2 * last + origin // shards, origin % shards

        @pl.when(jnp.logical_or(section != aa, shard != ba))
        def _():
            heard(aa, ba, origin)

    result = landing[0]
    for origin in range(1, 2 * shards):
        result = result + landing[origin]
    out[...] = result


def solution(mesh):
    sections, shards = mesh.shape["aa"], mesh.shape["ba"]

    def local(
        patches,
        token_first,
        token_second,
        channel_first,
        channel_second,
        gains,
        final_gain,
        head_weight,
        depths,
        widths,
        labels,
    ):
        images, patch_count, model = patches.shape
        candidates = depths.shape[0]
        slots = candidates // 2 * images
        lanes = pl.cdiv(candidates, 128) * 128
        vmem = pl.BlockSpec(memory_space=pltpu.VMEM)
        hbm = pl.BlockSpec(memory_space=pltpu.HBM)
        bf16 = jnp.bfloat16
        dma = pltpu.SemaphoreType.DMA
        line = pl.pallas_call(
            functools.partial(kernel, sections, shards),
            out_shape=jax.ShapeDtypeStruct((1, lanes), jnp.float32),
            in_specs=[hbm] * 11,
            out_specs=vmem,
            scratch_shapes=[
                pltpu.SMEM(depths.shape[::-1], jnp.int32),
                pltpu.SMEM(widths.shape[::-1], jnp.int32),
                pltpu.SMEM(labels.shape, jnp.int32),
                pltpu.VMEM(patches.shape, bf16),
                pltpu.VMEM((1, model), jnp.float32),
                pltpu.VMEM((slots, patch_count, model), bf16),
                pltpu.VMEM((2 * slots, patch_count, model), bf16),
                pltpu.VMEM(((QUARTERS + 1) * QUARTERS, patch_count, model), bf16),
                pltpu.VMEM((2,) + token_first.shape[1:], bf16),
                pltpu.VMEM((2,) + token_second.shape[1:], bf16),
                pltpu.VMEM((2, token_first.shape[2], patch_count), bf16),
                pltpu.VMEM((2,) + channel_first.shape[1:], bf16),
                pltpu.VMEM((2,) + channel_second.shape[1:], bf16),
                pltpu.VMEM((2,) + gains.shape[1:], jnp.float32),
                pltpu.VMEM(head_weight.shape[::-1], bf16),
                pltpu.VMEM((slots, model), jnp.float32),
                pltpu.VMEM((1, lanes), jnp.float32),
                pltpu.VMEM((2 * shards, 1, lanes), jnp.float32),
                dma((11,)),
                dma((3,)),
                dma((3,)),
                dma((4, QUARTERS, PARTS, 2)),
                dma((TEAM, QUARTERS, PARTS, 2)),
                dma((2 * slots,)),
                dma((slots,)),
                dma((sections * shards,)),
                dma((2 * shards,)),
            ],
            compiler_params=pltpu.CompilerParams(
                collective_id=0,
                has_side_effects=True,
                vmem_limit_bytes=58 * 1024 * 1024,
            ),
        )(
            depths.T,
            widths.T,
            labels,
            patches,
            gains,
            token_first,
            token_second,
            channel_first,
            channel_second,
            final_gain[None, :],
            head_weight.T,
        )
        return line[0, :candidates]

    return jax.shard_map(
        local,
        mesh=mesh,
        in_specs=(
            P("ba", None, None),
            P("aa", None, None),
            P("aa", None, None),
            P("aa", None, None),
            P("aa", None, None),
            P("aa", None, None),
            P(),
            P(),
            P(),
            P(),
            P("ba"),
        ),
        out_specs=P(),
        check_vma=False,
    )
```

```python
import functools

import jax
import jax.numpy as jnp
from jax import lax
from jax.experimental import pallas as pl
from jax.experimental.pallas import tpu as pltpu
from jax.sharding import PartitionSpec as P

UNIT = 4
QUARTERS = 4
TEAM = 4
PARTS = 2
LAG = 2
AHEAD = 2
MESH = pl.DeviceIdType.MESH
GELU_A = 0.7978845608028654
GELU_B = 0.044715 * GELU_A


def layer_norm(values, gain):
    center = values - jnp.mean(values, axis=-1, keepdims=True)
    spread = jnp.mean(center * center, axis=-1, keepdims=True)
    return center * lax.rsqrt(spread + 1e-06) * gain


def quick_norm(values, gain, pivot=None):
    if pivot is not None:
        values = values - pivot
    mean = jnp.mean(values, axis=-1, keepdims=True)
    square = jnp.mean(values * values, axis=-1, keepdims=True)
    spread = jnp.maximum(square - mean * mean, 0.0)
    return (values - mean) * lax.rsqrt(spread + 1e-06) * gain, mean


def gelu(x, half):
    x = x.astype(jnp.bfloat16)
    bent = jnp.tanh(x * (jnp.bfloat16(GELU_A) + jnp.bfloat16(GELU_B) * (x * x)))
    scaled = x * half
    return scaled + scaled * bent


def dot(a, b):
    return jnp.dot(a, b, preferred_element_type=jnp.float32)


def token_mix(floats, gain, token_one_t, token_two, quick=False):
    model = floats[0].shape[1]
    if quick:
        pairs = [quick_norm(value, gain) for value in floats]
        normed = [norm for norm, _ in pairs]
        means = jnp.concatenate([mean for _, mean in pairs], axis=0)
    else:
        normed = [layer_norm(value, gain) for value in floats]
        means = None
    normed = jnp.concatenate([norm.astype(jnp.bfloat16) for norm in normed], axis=1)
    hidden = gelu(dot(token_one_t, normed), jnp.bfloat16(0.5))
    part = dot(token_two, hidden)
    mixed = jnp.concatenate(
        [
            value + part[:, unit * model : (unit + 1) * model]
            for unit, value in enumerate(floats)
        ],
        axis=0,
    )
    return (mixed, means) if quick else mixed


def kernel(
    sections,
    shards,
    depths_in,
    widths_in,
    labels_in,
    patches_in,
    gains,
    token_first,
    token_second,
    channel_first,
    channel_second,
    final_gain_in,
    head_weight_t,
    out,
    depths,
    widths,
    labels,
    patches,
    final_gain,
    inbox,
    outbox,
    options,
    token_one,
    token_two,
    token_one_t,
    channel_one,
    channel_two,
    gain_pair,
    head,
    pooled,
    share,
    landing,
    load_sem,
    small_send,
    small_recv,
    weight_send,
    weight_recv,
    state_send,
    state_recv,
    share_send,
    landing_sem,
    turn_sem,
):
    section = lax.axis_index("aa")
    shard = lax.axis_index("ba")
    pair = section // 2
    side = section % 2
    pairs = sections // 2
    last = pairs - 1
    images, patch_count, model = patches_in.shape
    candidates = depths_in.shape[1]
    per = candidates // 2
    slots = per * images
    hidden_units = channel_first.shape[2]
    quarter = hidden_units // QUARTERS
    partner = section + 1 - 2 * side
    rank = shard % TEAM
    team = shard - rank
    beside = team + rank + 1 - 2 * (rank % 2)
    across = team + (rank + 2) % TEAM

    loads = [
        pltpu.make_async_copy(source.at[0], target.at[side], load_sem.at[index])
        for index, (source, target) in enumerate(
            (
                (token_first, token_one),
                (token_second, token_two),
                (channel_first, channel_one),
                (channel_second, channel_two),
                (gains, gain_pair),
            )
        )
    ]
    head_load = pltpu.make_async_copy(head_weight_t, head, load_sem.at[5])
    tables = [
        pltpu.make_async_copy(source, target, load_sem.at[6 + index])
        for index, (source, target) in enumerate(
            (
                (patches_in, patches),
                (depths_in, depths),
                (widths_in, widths),
                (labels_in, labels),
                (final_gain_in, final_gain),
            )
        )
    ]
    loads = loads + tables
    for load in loads:
        load.start()

    @pl.when(pair == last)
    def _():
        head_load.start()

    barrier = pltpu.get_barrier_semaphore()

    def greet(aa, ba):
        pl.semaphore_signal(barrier, inc=1, device_id=(aa, ba), device_id_type=MESH)

    @pl.when(pair == 0)
    def _():
        greet(partner, shard)

    @pl.when(pair == 1)
    def _():
        greet(side, shard)

    @pl.when(pair > 0)
    def _():
        greet(partner, shard)
        greet(section, beside)
        greet(section, across)

    @pl.when(pair > 1)
    def _():
        greet(section - 2, shard)

    def greet_last(target, carry):
        aa, ba = 2 * last + target // shards, target % shards

        @pl.when(jnp.logical_or(aa != section, ba != shard))
        def _():
            greet(aa, ba)

        return carry

    lax.fori_loop(0, 2 * shards, greet_last, 0)

    @pl.when(section == 1)
    def _():
        pl.semaphore_wait(barrier, 2)

    @pl.when(jnp.logical_and(pair > 0, pair < last))
    def _():
        pl.semaphore_wait(barrier, 4)

    @pl.when(pair == last)
    def _():
        pl.semaphore_wait(barrier, sections * shards + 2)

    def state_copy(source, target, aa):
        return pltpu.make_async_remote_copy(
            src_ref=outbox.at[source],
            dst_ref=inbox.at[target],
            send_sem=state_send.at[source],
            recv_sem=state_recv.at[target],
            device_id=(aa, shard),
            device_id_type=MESH,
        )

    def arrived(slot):
        state_copy(slot, slot, section).wait_recv()

    @pl.when(section == 0)
    def _():
        for load in loads:
            load.wait()
        floats = [patches[image].astype(jnp.float32) for image in range(images)]
        mixed = token_mix(floats, gain_pair[0, 0:1, :], token_one[0].T, token_two[0])
        second = layer_norm(mixed, gain_pair[0, 1:2, :]).astype(jnp.bfloat16)
        total = mixed
        for width in range(QUARTERS):
            cut = slice(width * quarter, (width + 1) * quarter)
            hidden = gelu(dot(second, channel_one[0, :, cut]), jnp.bfloat16(0.5))
            total = total + dot(hidden, channel_two[0, cut, :])
            rounded = total.astype(jnp.bfloat16)
            for image in range(images):
                slot = image * QUARTERS + width
                outbox[slot] = rounded[image * patch_count : (image + 1) * patch_count]
        pl.semaphore_wait(barrier, 2)
        for slot in range(images * QUARTERS):
            state_copy(slot, slot, 1).start()

        def relay(slot):
            return pltpu.make_async_remote_copy(
                src_ref=inbox.at[slot],
                dst_ref=inbox.at[slot],
                send_sem=state_send.at[slots + slot],
                recv_sem=state_recv.at[slot],
                device_id=(2, shard),
                device_id_type=MESH,
            )

        def pass_on(slot, carry):
            arrived(slot)
            relay(slot).start()
            return carry

        def drain(slot, carry):
            relay(slot).wait_send()
            return carry

        lax.fori_loop(0, slots, pass_on, 0)
        lax.fori_loop(0, slots, drain, 0)
        for slot in range(images * QUARTERS):
            state_copy(slot, slot, 1).wait_send()

    @pl.when(section == 1)
    def _():
        for load in loads:
            load.wait()

        def image_step(image, carry):
            base = image * QUARTERS
            for width in range(QUARTERS):
                arrived(base + width)
            states = [inbox[base + width] for width in range(QUARTERS)]
            floats = [state.astype(jnp.float32) for state in states]
            mixed = token_mix(
                floats, gain_pair[1, 0:1, :], token_one[1].T, token_two[1]
            )
            second = layer_norm(mixed, gain_pair[1, 1:2, :]).astype(jnp.bfloat16)
            total = mixed
            for first in range(QUARTERS):
                options[first] = states[first]
            for width in range(QUARTERS):
                cut = slice(width * quarter, (width + 1) * quarter)
                hidden = gelu(dot(second, channel_one[1, :, cut]), jnp.bfloat16(0.5))
                total = total + dot(hidden, channel_two[1, cut, :])
                rounded = total.astype(jnp.bfloat16)
                for first in range(QUARTERS):
                    options[(width + 1) * QUARTERS + first] = rounded[
                        first * patch_count : (first + 1) * patch_count
                    ]

            def pick(index, carry):
                for parity in range(2):
                    candidate = 2 * index + parity
                    active = 1 < depths[0, candidate]
                    chosen = jnp.where(active, widths[1, candidate], 0)
                    row = chosen * QUARTERS + jnp.maximum(widths[0, candidate], 1) - 1
                    slot = image * per + index
                    outbox[parity * slots + slot] = options[row]
                    state_copy(parity * slots + slot, slot, 3 * parity).start()
                return carry

            lax.fori_loop(0, per, pick, 0)
            return carry

        lax.fori_loop(0, images, image_step, 0)

        def drain(index, carry):
            state_copy(index, index % slots, 2).wait_send()
            return carry

        lax.fori_loop(0, 2 * slots, drain, 0)

    rounds = QUARTERS

    def region(turn, owner, part):
        spans = []
        for height in (model, hidden_units):
            rows = height // (rounds * TEAM * PARTS)
            start = ((turn * TEAM + owner) * PARTS + part) * rows
            spans.append((pl.ds(pl.multiple_of(start, rows), rows), slice(None)))
        return spans

    def weight_copy(parity, from_input, kind, turn, part, owner, aa, ba, which):
        rows, columns = region(turn, owner, part)[which]
        target = (channel_one, channel_two)[which].at[parity, rows, columns]
        if from_input:
            ref = (channel_first, channel_second)[which].at[0, rows, columns]
        else:
            ref = target
        return pltpu.make_async_remote_copy(
            src_ref=ref,
            dst_ref=target,
            send_sem=weight_send.at[kind, turn, part, which],
            recv_sem=weight_recv.at[owner, turn, part, which],
            device_id=(aa, ba),
            device_id_type=MESH,
        )

    other = 1 - side

    def small_copies(part):
        return [
            pltpu.make_async_remote_copy(
                src_ref=source.at[0],
                dst_ref=target.at[part],
                send_sem=small_send.at[index],
                recv_sem=small_recv.at[index],
                device_id=(partner, shard),
                device_id_type=MESH,
            )
            for index, (source, target) in enumerate(
                (
                    (token_first, token_one),
                    (token_second, token_two),
                    (gains, gain_pair),
                )
            )
        ]

    rank_beside = rank + 1 - 2 * (rank % 2)
    rank_across = (rank + 2) % TEAM
    rank_far = (rank_beside + 2) % TEAM

    def to_partner(turn, part, which):
        return weight_copy(side, True, 0, turn, part, rank, partner, shard, which)

    def to_across(turn, part, which):
        return weight_copy(other, False, 1, turn, part, rank, section, across, which)

    def to_beside(turn, part, which):
        return weight_copy(other, False, 2, turn, part, rank, section, beside, which)

    def to_beside_again(turn, part, which):
        return weight_copy(
            other, False, 3, turn, part, rank_across, section, beside, which
        )

    def from_owner(turn, owner, part, which):
        return weight_copy(other, False, 0, turn, part, owner, section, shard, which)

    def for_parts(act):
        def visit(index, carry):
            for which in range(2):
                act(index // PARTS, index % PARTS, which)
            return carry

        lax.fori_loop(0, rounds * PARTS, visit, 0)

    def section_step(group, first, finish, parity, states):
        here = 2 * pair + parity
        floats = [state.astype(jnp.float32) for state in states]
        mixed, means = token_mix(
            floats,
            gain_pair[parity, 0:1, :],
            token_one_t[parity],
            token_two[parity],
            quick=True,
        )
        second, _ = quick_norm(mixed, gain_pair[parity, 1:2, :], means)
        second = second.astype(jnp.bfloat16)
        pre = dot(second, channel_one[parity])
        lane = lax.broadcasted_iota(jnp.int32, (1, hidden_units), 1)
        parts = []
        actives = []
        for unit in range(group):
            candidate = 2 * ((first + unit) % per) + side
            actives.append(here % UNIT < depths[here // UNIT, candidate])
            half = jnp.where(lane < widths[here, candidate] * quarter, 0.5, 0.0).astype(
                jnp.bfloat16
            )
            rows = slice(unit * patch_count, (unit + 1) * patch_count)
            parts.append(gelu(pre[rows], half))
        hidden = jnp.concatenate(parts, axis=0)
        total = (mixed + dot(hidden, channel_two[parity])).astype(jnp.bfloat16)
        return [
            jnp.where(
                actives[unit],
                total[unit * patch_count : (unit + 1) * patch_count],
                states[unit],
            )
            for unit in range(group)
        ]

    def pool(source, row):
        final = layer_norm(outbox[source].astype(jnp.float32), final_gain[...])
        pooled[pl.ds(row, 1), :] = jnp.mean(final, axis=0, keepdims=True)

    def chunk(group, finish, index, carry):
        first = index * group
        for unit in range(group):
            arrived(first + unit)

        def both(parity, carry):
            states = [inbox[first + unit] for unit in range(group)]
            updated = section_step(group, first, finish, parity, states)
            if finish:
                unit = jnp.minimum(parity, group - 1)
                row = jnp.where(index == 0, slots, first - group) + unit
                pool(row, row)
            for unit in range(group):
                outbox[first + unit] = updated[unit]

            @pl.when(parity == 0)
            def _():
                for unit in range(group):
                    inbox[first + unit] = updated[unit]

                @pl.when((pair == 1) & (index == 0) & (rank % 2 == 0))
                def _():
                    pl.semaphore_signal(
                        turn_sem,
                        inc=1,
                        device_id=(section, beside),
                        device_id_type=MESH,
                    )

            return carry

        lax.fori_loop(0, 2, both, 0)
        if not finish:
            for unit in range(group):
                state_copy(first + unit, first + unit, section + 2).start()
        return carry

    @pl.when(pair > 0)
    def _():
        for copy in small_copies(side):
            copy.start()
        for index in range(AHEAD):
            for which in range(2):
                to_partner(index // PARTS, index % PARTS, which).start()

        for load in loads:
            load.wait()
        token_one_t[side] = token_one[side].T
        for copy in small_copies(other):
            copy.wait_recv()
        token_one_t[other] = token_one[other].T
        def forward(turn, part, which):
            from_owner(turn, rank, part, which).wait_recv()
            to_across(turn, part, which).start()
            to_beside(turn, part, which).start()
            follow = turn * PARTS + part + AHEAD

            @pl.when(follow < rounds * PARTS)
            def _():
                to_partner(follow // PARTS, follow % PARTS, which).start()

            before = turn * PARTS + part - LAG
            if which == 1:

                @pl.when(before >= 0)
                def _():
                    forward_again(before)

        def forward_again(index):
            turn, part = index // PARTS, index % PARTS
            for which in range(2):
                from_owner(turn, rank_across, part, which).wait_recv()
                to_beside_again(turn, part, which).start()

        def finish(turn, part, which):
            from_owner(turn, rank_beside, part, which).wait_recv()
            from_owner(turn, rank_far, part, which).wait_recv()

        for_parts(forward)
        for index in range(rounds * PARTS - LAG, rounds * PARTS):
            forward_again(index)
        for_parts(finish)
        group = 2 if slots % 2 == 0 else 1

        @pl.when((pair == 1) & (rank % 2 == 1))
        def _():
            pl.semaphore_wait(turn_sem, 1)

        steps = slots // group

        @pl.when(pair < last)
        def _():
            lax.fori_loop(0, steps, functools.partial(chunk, group, False), 0)

        @pl.when(pair == last)
        def _():
            for unit in range(group):
                outbox[slots + unit] = jnp.zeros((patch_count, model), jnp.bfloat16)
            lax.fori_loop(0, steps, functools.partial(chunk, group, True), 0)
            for unit in range(group):
                pool(slots - group + unit, slots - group + unit)

        for copy in small_copies(side):
            copy.wait_send()
        def settle(turn, part, which):
            for copy in (to_partner, to_across, to_beside, to_beside_again):
                copy(turn, part, which).wait_send()

        for_parts(settle)

    @pl.when(jnp.logical_and(pair > 0, pair < last))
    def _():
        def drain(slot, carry):
            state_copy(slot, slot, section + 2).wait_send()
            return carry

        lax.fori_loop(0, slots, drain, 0)

    def tell(aa, ba):
        mine = side * shards + shard
        return pltpu.make_async_remote_copy(
            src_ref=share,
            dst_ref=landing.at[mine],
            send_sem=share_send.at[aa * shards + ba],
            recv_sem=landing_sem.at[mine],
            device_id=(aa, ba),
            device_id_type=MESH,
        )

    def each_other(act):
        def visit(target, carry):
            aa, ba = target // shards, target % shards

            @pl.when(jnp.logical_or(aa != section, ba != shard))
            def _():
                act(tell(aa, ba))

            return carry

        lax.fori_loop(0, sections * shards, visit, 0)

    def heard(aa, ba, origin):
        pltpu.make_async_remote_copy(
            src_ref=share,
            dst_ref=landing.at[origin],
            send_sem=share_send.at[0],
            recv_sem=landing_sem.at[origin],
            device_id=(aa, ba),
            device_id_type=MESH,
        ).wait_recv()

    @pl.when(pair == last)
    def _():
        head_load.wait()
        logits = lax.dot_general(
            pooled[:slots].astype(jnp.bfloat16),
            head[...],
            (((1,), (1,)), ((), ())),
            preferred_element_type=jnp.float32,
        )
        top = jnp.max(logits, axis=-1, keepdims=True)
        total = top + jnp.log(jnp.sum(jnp.exp(logits - top), axis=-1, keepdims=True))
        rows = lax.broadcasted_iota(jnp.int32, logits.shape, 0)
        classes = lax.broadcasted_iota(jnp.int32, logits.shape, 1)
        wanted = jnp.full(logits.shape, labels[0], jnp.int32)
        for image in range(1, images):
            wanted = jnp.where(rows >= image * per, labels[image], wanted)
        picked = jnp.sum(
            jnp.where(classes == wanted, logits, 0.0), axis=-1, keepdims=True
        )
        losses = total - picked
        summed = losses[:per]
        for image in range(1, images):
            summed = summed + losses[image * per : (image + 1) * per]
        lanes = out.shape[1]
        rows = lax.broadcasted_iota(jnp.int32, (per, lanes), 0)
        cols = lax.broadcasted_iota(jnp.int32, (per, lanes), 1)
        spread = jnp.broadcast_to(summed, (per, lanes))
        line = jnp.sum(
            jnp.where(2 * rows + side == cols, spread, 0.0), axis=0, keepdims=True
        )
        share[...] = line
        landing[side * shards + shard] = line
        each_other(lambda copy: copy.start())
        each_other(lambda copy: copy.wait_send())

    for origin in range(2 * shards):
        aa, ba = 2 * last + origin // shards, origin % shards

        @pl.when(jnp.logical_or(section != aa, shard != ba))
        def _():
            heard(aa, ba, origin)

    result = landing[0]
    for origin in range(1, 2 * shards):
        result = result + landing[origin]
    out[...] = result


def solution(mesh):
    sections, shards = mesh.shape["aa"], mesh.shape["ba"]

    def local(
        patches,
        token_first,
        token_second,
        channel_first,
        channel_second,
        gains,
        final_gain,
        head_weight,
        depths,
        widths,
        labels,
    ):
        images, patch_count, model = patches.shape
        candidates = depths.shape[0]
        slots = candidates // 2 * images
        lanes = pl.cdiv(candidates, 128) * 128
        vmem = pl.BlockSpec(memory_space=pltpu.VMEM)
        hbm = pl.BlockSpec(memory_space=pltpu.HBM)
        bf16 = jnp.bfloat16
        dma = pltpu.SemaphoreType.DMA
        line = pl.pallas_call(
            functools.partial(kernel, sections, shards),
            out_shape=jax.ShapeDtypeStruct((1, lanes), jnp.float32),
            in_specs=[hbm] * 11,
            out_specs=vmem,
            scratch_shapes=[
                pltpu.SMEM(depths.shape[::-1], jnp.int32),
                pltpu.SMEM(widths.shape[::-1], jnp.int32),
                pltpu.SMEM(labels.shape, jnp.int32),
                pltpu.VMEM(patches.shape, bf16),
                pltpu.VMEM((1, model), jnp.float32),
                pltpu.VMEM((slots, patch_count, model), bf16),
                pltpu.VMEM((2 * slots, patch_count, model), bf16),
                pltpu.VMEM(((QUARTERS + 1) * QUARTERS, patch_count, model), bf16),
                pltpu.VMEM((2,) + token_first.shape[1:], bf16),
                pltpu.VMEM((2,) + token_second.shape[1:], bf16),
                pltpu.VMEM((2, token_first.shape[2], patch_count), bf16),
                pltpu.VMEM((2,) + channel_first.shape[1:], bf16),
                pltpu.VMEM((2,) + channel_second.shape[1:], bf16),
                pltpu.VMEM((2,) + gains.shape[1:], jnp.float32),
                pltpu.VMEM(head_weight.shape[::-1], bf16),
                pltpu.VMEM((slots + 8, model), jnp.float32),
                pltpu.VMEM((1, lanes), jnp.float32),
                pltpu.VMEM((2 * shards, 1, lanes), jnp.float32),
                dma((11,)),
                dma((3,)),
                dma((3,)),
                dma((4, QUARTERS, PARTS, 2)),
                dma((TEAM, QUARTERS, PARTS, 2)),
                dma((2 * slots,)),
                dma((slots,)),
                dma((sections * shards,)),
                dma((2 * shards,)),
                pltpu.SemaphoreType.REGULAR,
            ],
            compiler_params=pltpu.CompilerParams(
                collective_id=0,
                has_side_effects=True,
                vmem_limit_bytes=58 * 1024 * 1024,
            ),
        )(
            depths.T,
            widths.T,
            labels,
            patches,
            gains,
            token_first,
            token_second,
            channel_first,
            channel_second,
            final_gain[None, :],
            head_weight.T,
        )
        return line[0, :candidates]

    return jax.shard_map(
        local,
        mesh=mesh,
        in_specs=(
            P("ba", None, None),
            P("aa", None, None),
            P("aa", None, None),
            P("aa", None, None),
            P("aa", None, None),
            P("aa", None, None),
            P(),
            P(),
            P(),
            P(),
            P("ba"),
        ),
        out_specs=P(),
        check_vma=False,
    )
```

```python
import functools

import jax
import jax.numpy as jnp
from jax import lax
from jax.experimental import pallas as pl
from jax.experimental.pallas import tpu as pltpu
from jax.sharding import PartitionSpec as P

UNIT = 4
QUARTERS = 4
TEAM = 4
PARTS = 2
LAG = 2
AHEAD = 2
MESH = pl.DeviceIdType.MESH
GELU_A = 0.7978845608028654
GELU_B = 0.044715 * GELU_A


def layer_norm(values, gain):
    center = values - jnp.mean(values, axis=-1, keepdims=True)
    spread = jnp.mean(center * center, axis=-1, keepdims=True)
    return center * lax.rsqrt(spread + 1e-06) * gain


def quick_norm(values, gain, pivot=None):
    if pivot is not None:
        values = values - pivot
    mean = jnp.mean(values, axis=-1, keepdims=True)
    square = jnp.mean(values * values, axis=-1, keepdims=True)
    spread = jnp.maximum(square - mean * mean, 0.0)
    return (values - mean) * lax.rsqrt(spread + 1e-06) * gain, mean


def gelu(x, half):
    x = x.astype(jnp.bfloat16)
    bent = jnp.tanh(x * (jnp.bfloat16(GELU_A) + jnp.bfloat16(GELU_B) * (x * x)))
    scaled = x * half
    return scaled + scaled * bent


def dot(a, b):
    return jnp.dot(a, b, preferred_element_type=jnp.float32)


def token_mix(floats, gain, token_one_t, token_two, quick=False):
    model = floats[0].shape[1]
    if quick:
        pairs = [quick_norm(value, gain) for value in floats]
        normed = [norm for norm, _ in pairs]
        means = jnp.concatenate([mean for _, mean in pairs], axis=0)
    else:
        normed = [layer_norm(value, gain) for value in floats]
        means = None
    normed = jnp.concatenate([norm.astype(jnp.bfloat16) for norm in normed], axis=1)
    hidden = gelu(dot(token_one_t, normed), jnp.bfloat16(0.5))
    part = dot(token_two, hidden)
    mixed = jnp.concatenate(
        [
            value + part[:, unit * model : (unit + 1) * model]
            for unit, value in enumerate(floats)
        ],
        axis=0,
    )
    return (mixed, means) if quick else mixed


def token_mix_rows(rows, units, gain, token_one_wide, token_two):
    normed, means = quick_norm(rows, gain)
    hidden = gelu(dot(token_one_wide, normed.astype(jnp.bfloat16)), jnp.bfloat16(0.5))
    height = hidden.shape[0] // units
    part = [
        dot(token_two, hidden[unit * height : (unit + 1) * height])
        for unit in range(units)
    ]
    return rows + jnp.concatenate(part, axis=0), means


def diagonal(block, count):
    zero = jnp.zeros_like(block)
    return jnp.concatenate(
        [
            jnp.concatenate(
                [block if row == column else zero for column in range(count)], axis=1
            )
            for row in range(count)
        ],
        axis=0,
    )


def kernel(
    sections,
    shards,
    depths_in,
    widths_in,
    labels_in,
    patches_in,
    gains,
    token_first,
    token_second,
    channel_first,
    channel_second,
    final_gain_in,
    head_weight_t,
    out,
    depths,
    widths,
    labels,
    patches,
    final_gain,
    inbox,
    outbox,
    options,
    token_one,
    token_two,
    token_one_t,
    channel_one,
    channel_two,
    gain_pair,
    head,
    pooled,
    share,
    landing,
    load_sem,
    small_send,
    small_recv,
    weight_send,
    weight_recv,
    state_send,
    state_recv,
    share_send,
    landing_sem,
    turn_sem,
):
    section = lax.axis_index("aa")
    shard = lax.axis_index("ba")
    pair = section // 2
    side = section % 2
    pairs = sections // 2
    last = pairs - 1
    images, patch_count, model = patches_in.shape
    candidates = depths_in.shape[1]
    per = candidates // 2
    slots = per * images
    hidden_units = channel_first.shape[2]
    quarter = hidden_units // QUARTERS
    partner = section + 1 - 2 * side
    rank = shard % TEAM
    team = shard - rank
    beside = team + rank + 1 - 2 * (rank % 2)
    across = team + (rank + 2) % TEAM

    loads = [
        pltpu.make_async_copy(source.at[0], target.at[side], load_sem.at[index])
        for index, (source, target) in enumerate(
            (
                (token_first, token_one),
                (token_second, token_two),
                (channel_first, channel_one),
                (channel_second, channel_two),
                (gains, gain_pair),
            )
        )
    ]
    head_load = pltpu.make_async_copy(head_weight_t, head, load_sem.at[5])
    tables = [
        pltpu.make_async_copy(source, target, load_sem.at[6 + index])
        for index, (source, target) in enumerate(
            (
                (patches_in, patches),
                (depths_in, depths),
                (widths_in, widths),
                (labels_in, labels),
                (final_gain_in, final_gain),
            )
        )
    ]
    loads = loads + tables
    barrier = pltpu.get_barrier_semaphore()

    def greet(aa, ba):
        pl.semaphore_signal(barrier, inc=1, device_id=(aa, ba), device_id_type=MESH)

    @pl.when(pair == 0)
    def _():
        greet(partner, shard)

    @pl.when(pair == 1)
    def _():
        greet(side, shard)

    @pl.when(pair > 0)
    def _():
        greet(partner, shard)
        greet(section, beside)
        greet(section, across)

    @pl.when(pair > 1)
    def _():
        greet(section - 2, shard)

    for load in loads:
        load.start()

    @pl.when(pair == last)
    def _():
        head_load.start()

    def greet_last(target, carry):
        aa, ba = 2 * last + target // shards, target % shards

        @pl.when(jnp.logical_or(aa != section, ba != shard))
        def _():
            greet(aa, ba)

        return carry

    lax.fori_loop(0, 2 * shards, greet_last, 0)

    @pl.when(section == 1)
    def _():
        pl.semaphore_wait(barrier, 2)

    @pl.when(jnp.logical_and(pair > 0, pair < last))
    def _():
        pl.semaphore_wait(barrier, 4)

    @pl.when(pair == last)
    def _():
        pl.semaphore_wait(barrier, sections * shards + 2)

    def state_copy(source, target, aa):
        return pltpu.make_async_remote_copy(
            src_ref=outbox.at[source],
            dst_ref=inbox.at[target],
            send_sem=state_send.at[source],
            recv_sem=state_recv.at[target],
            device_id=(aa, shard),
            device_id_type=MESH,
        )

    def arrived(slot):
        state_copy(slot, slot, section).wait_recv()

    @pl.when(section == 0)
    def _():
        for load in loads:
            load.wait()
        floats = [patches[image].astype(jnp.float32) for image in range(images)]
        mixed = token_mix(floats, gain_pair[0, 0:1, :], token_one[0].T, token_two[0])
        second = layer_norm(mixed, gain_pair[0, 1:2, :]).astype(jnp.bfloat16)
        total = mixed
        for width in range(QUARTERS):
            cut = slice(width * quarter, (width + 1) * quarter)
            hidden = gelu(dot(second, channel_one[0, :, cut]), jnp.bfloat16(0.5))
            total = total + dot(hidden, channel_two[0, cut, :])
            rounded = total.astype(jnp.bfloat16)
            for image in range(images):
                slot = image * QUARTERS + width
                outbox[slot] = rounded[image * patch_count : (image + 1) * patch_count]
        pl.semaphore_wait(barrier, 2)
        for slot in range(images * QUARTERS):
            state_copy(slot, slot, 1).start()

        def relay(slot):
            return pltpu.make_async_remote_copy(
                src_ref=inbox.at[slot],
                dst_ref=inbox.at[slot],
                send_sem=state_send.at[slots + slot],
                recv_sem=state_recv.at[slot],
                device_id=(2, shard),
                device_id_type=MESH,
            )

        def pass_on(slot, carry):
            arrived(slot)
            relay(slot).start()
            return carry

        def drain(slot, carry):
            relay(slot).wait_send()
            return carry

        lax.fori_loop(0, slots, pass_on, 0)
        lax.fori_loop(0, slots, drain, 0)
        for slot in range(images * QUARTERS):
            state_copy(slot, slot, 1).wait_send()

    @pl.when(section == 1)
    def _():
        for load in loads:
            load.wait()

        def image_step(image, carry):
            base = image * QUARTERS
            for width in range(QUARTERS):
                arrived(base + width)
            states = [inbox[base + width] for width in range(QUARTERS)]
            floats = [state.astype(jnp.float32) for state in states]
            mixed = token_mix(
                floats, gain_pair[1, 0:1, :], token_one[1].T, token_two[1]
            )
            second = layer_norm(mixed, gain_pair[1, 1:2, :]).astype(jnp.bfloat16)
            total = mixed
            for first in range(QUARTERS):
                options[first] = states[first]
            for width in range(QUARTERS):
                cut = slice(width * quarter, (width + 1) * quarter)
                hidden = gelu(dot(second, channel_one[1, :, cut]), jnp.bfloat16(0.5))
                total = total + dot(hidden, channel_two[1, cut, :])
                rounded = total.astype(jnp.bfloat16)
                for first in range(QUARTERS):
                    options[(width + 1) * QUARTERS + first] = rounded[
                        first * patch_count : (first + 1) * patch_count
                    ]

            def pick(index, carry):
                for parity in range(2):
                    candidate = 2 * index + parity
                    active = 1 < depths[0, candidate]
                    chosen = jnp.where(active, widths[1, candidate], 0)
                    row = chosen * QUARTERS + jnp.maximum(widths[0, candidate], 1) - 1
                    slot = image * per + index
                    outbox[parity * slots + slot] = options[row]
                    state_copy(parity * slots + slot, slot, 3 * parity).start()
                return carry

            lax.fori_loop(0, per, pick, 0)
            return carry

        lax.fori_loop(0, images, image_step, 0)

        def drain(index, carry):
            state_copy(index, index % slots, 2).wait_send()
            return carry

        lax.fori_loop(0, 2 * slots, drain, 0)

    rounds = QUARTERS
    group = 2 if slots % 2 == 0 else 1

    def region(turn, owner, part):
        spans = []
        for height in (model, hidden_units):
            rows = height // (rounds * TEAM * PARTS)
            start = ((turn * TEAM + owner) * PARTS + part) * rows
            spans.append((pl.ds(pl.multiple_of(start, rows), rows), slice(None)))
        return spans

    def weight_copy(parity, from_input, kind, turn, part, owner, aa, ba, which):
        rows, columns = region(turn, owner, part)[which]
        target = (channel_one, channel_two)[which].at[parity, rows, columns]
        if from_input:
            ref = (channel_first, channel_second)[which].at[0, rows, columns]
        else:
            ref = target
        return pltpu.make_async_remote_copy(
            src_ref=ref,
            dst_ref=target,
            send_sem=weight_send.at[kind, turn, part, which],
            recv_sem=weight_recv.at[owner, turn, part, which],
            device_id=(aa, ba),
            device_id_type=MESH,
        )

    other = 1 - side

    def small_copies(part):
        return [
            pltpu.make_async_remote_copy(
                src_ref=source.at[0],
                dst_ref=target.at[part],
                send_sem=small_send.at[index],
                recv_sem=small_recv.at[index],
                device_id=(partner, shard),
                device_id_type=MESH,
            )
            for index, (source, target) in enumerate(
                (
                    (token_first, token_one),
                    (token_second, token_two),
                    (gains, gain_pair),
                )
            )
        ]

    rank_beside = rank + 1 - 2 * (rank % 2)
    rank_across = (rank + 2) % TEAM
    rank_far = (rank_beside + 2) % TEAM

    def to_partner(turn, part, which):
        return weight_copy(side, True, 0, turn, part, rank, partner, shard, which)

    def to_across(turn, part, which):
        return weight_copy(other, False, 1, turn, part, rank, section, across, which)

    def to_beside(turn, part, which):
        return weight_copy(other, False, 2, turn, part, rank, section, beside, which)

    def to_beside_again(turn, part, which):
        return weight_copy(
            other, False, 3, turn, part, rank_across, section, beside, which
        )

    def from_owner(turn, owner, part, which):
        return weight_copy(other, False, 0, turn, part, owner, section, shard, which)

    def for_parts(act):
        def visit(index, carry):
            for which in range(2):
                act(index // PARTS, index % PARTS, which)
            return carry

        lax.fori_loop(0, rounds * PARTS, visit, 0)

    def section_step(group, first, finish, parity, states):
        here = 2 * pair + parity
        mixed, means = token_mix_rows(
            jnp.concatenate(states, axis=0).astype(jnp.float32),
            group,
            gain_pair[parity, 0:1, :],
            token_one_t[parity],
            token_two[parity],
        )
        second, _ = quick_norm(mixed, gain_pair[parity, 1:2, :], means)
        second = second.astype(jnp.bfloat16)
        pre = dot(second, channel_one[parity])
        lane = lax.broadcasted_iota(jnp.int32, (1, hidden_units), 1)
        parts = []
        actives = []
        for unit in range(group):
            candidate = 2 * ((first + unit) % per) + side
            actives.append(here % UNIT < depths[here // UNIT, candidate])
            half = jnp.where(lane < widths[here, candidate] * quarter, 0.5, 0.0).astype(
                jnp.bfloat16
            )
            rows = slice(unit * patch_count, (unit + 1) * patch_count)
            parts.append(gelu(pre[rows], half))
        hidden = jnp.concatenate(parts, axis=0)
        total = (mixed + dot(hidden, channel_two[parity])).astype(jnp.bfloat16)
        return [
            jnp.where(
                actives[unit],
                total[unit * patch_count : (unit + 1) * patch_count],
                states[unit],
            )
            for unit in range(group)
        ]

    def pool(source, row):
        final = layer_norm(outbox[source].astype(jnp.float32), final_gain[...])
        pooled[pl.ds(row, 1), :] = jnp.mean(final, axis=0, keepdims=True)

    def chunk(group, finish, index, carry):
        first = index * group
        for unit in range(group):
            arrived(first + unit)

        def both(parity, carry):
            states = [inbox[first + unit] for unit in range(group)]
            updated = section_step(group, first, finish, parity, states)
            if finish:
                unit = jnp.minimum(parity, group - 1)
                row = jnp.where(index == 0, slots, first - group) + unit
                pool(row, row)
            for unit in range(group):
                outbox[first + unit] = updated[unit]

            @pl.when(parity == 0)
            def _():
                for unit in range(group):
                    inbox[first + unit] = updated[unit]

                @pl.when((pair == 1) & (index == 0) & (rank % 2 == 0))
                def _():
                    pl.semaphore_signal(
                        turn_sem,
                        inc=1,
                        device_id=(section, beside),
                        device_id_type=MESH,
                    )

            return carry

        lax.fori_loop(0, 2, both, 0)
        if not finish:
            for unit in range(group):
                state_copy(first + unit, first + unit, section + 2).start()
        return carry

    @pl.when(pair > 0)
    def _():
        for copy in small_copies(side):
            copy.start()
        for index in range(AHEAD):
            for which in range(2):
                to_partner(index // PARTS, index % PARTS, which).start()

        for load in loads:
            load.wait()
        token_one_t[side] = diagonal(token_one[side].T, group)
        for copy in small_copies(other):
            copy.wait_recv()
        token_one_t[other] = diagonal(token_one[other].T, group)
        def forward(turn, part, which):
            from_owner(turn, rank, part, which).wait_recv()
            to_across(turn, part, which).start()
            to_beside(turn, part, which).start()
            follow = turn * PARTS + part + AHEAD

            @pl.when(follow < rounds * PARTS)
            def _():
                to_partner(follow // PARTS, follow % PARTS, which).start()

            before = turn * PARTS + part - LAG
            if which == 1:

                @pl.when(before >= 0)
                def _():
                    forward_again(before)

        def forward_again(index):
            turn, part = index // PARTS, index % PARTS
            for which in range(2):
                from_owner(turn, rank_across, part, which).wait_recv()
                to_beside_again(turn, part, which).start()

        def finish(turn, part, which):
            from_owner(turn, rank_beside, part, which).wait_recv()
            from_owner(turn, rank_far, part, which).wait_recv()

        for_parts(forward)
        for index in range(rounds * PARTS - LAG, rounds * PARTS):
            forward_again(index)
        for_parts(finish)

        @pl.when((pair == 1) & (rank % 2 == 1))
        def _():
            pl.semaphore_wait(turn_sem, 1)

        steps = slots // group

        @pl.when(pair < last)
        def _():
            lax.fori_loop(0, steps, functools.partial(chunk, group, False), 0)

        @pl.when(pair == last)
        def _():
            for unit in range(group):
                outbox[slots + unit] = jnp.zeros((patch_count, model), jnp.bfloat16)
            lax.fori_loop(0, steps, functools.partial(chunk, group, True), 0)
            for unit in range(group):
                pool(slots - group + unit, slots - group + unit)

    @pl.when(jnp.logical_and(pair > 0, pair < last))
    def _():
        def drain(slot, carry):
            state_copy(slot, slot, section + 2).wait_send()
            return carry

        lax.fori_loop(0, slots, drain, 0)

    def tell(aa, ba):
        mine = side * shards + shard
        return pltpu.make_async_remote_copy(
            src_ref=share,
            dst_ref=landing.at[mine],
            send_sem=share_send.at[aa * shards + ba],
            recv_sem=landing_sem.at[mine],
            device_id=(aa, ba),
            device_id_type=MESH,
        )

    def each_other(act):
        def visit(target, carry):
            aa, ba = target // shards, target % shards

            @pl.when(jnp.logical_or(aa != section, ba != shard))
            def _():
                act(tell(aa, ba))

            return carry

        lax.fori_loop(0, sections * shards, visit, 0)

    def heard(aa, ba, origin):
        pltpu.make_async_remote_copy(
            src_ref=share,
            dst_ref=landing.at[origin],
            send_sem=share_send.at[0],
            recv_sem=landing_sem.at[origin],
            device_id=(aa, ba),
            device_id_type=MESH,
        ).wait_recv()

    @pl.when(pair == last)
    def _():
        head_load.wait()
        logits = lax.dot_general(
            pooled[:slots].astype(jnp.bfloat16),
            head[...],
            (((1,), (1,)), ((), ())),
            preferred_element_type=jnp.float32,
        )
        top = jnp.max(logits, axis=-1, keepdims=True)
        total = top + jnp.log(jnp.sum(jnp.exp(logits - top), axis=-1, keepdims=True))
        rows = lax.broadcasted_iota(jnp.int32, logits.shape, 0)
        classes = lax.broadcasted_iota(jnp.int32, logits.shape, 1)
        wanted = jnp.full(logits.shape, labels[0], jnp.int32)
        for image in range(1, images):
            wanted = jnp.where(rows >= image * per, labels[image], wanted)
        picked = jnp.sum(
            jnp.where(classes == wanted, logits, 0.0), axis=-1, keepdims=True
        )
        losses = total - picked
        summed = losses[:per]
        for image in range(1, images):
            summed = summed + losses[image * per : (image + 1) * per]
        lanes = out.shape[1]
        rows = lax.broadcasted_iota(jnp.int32, (per, lanes), 0)
        cols = lax.broadcasted_iota(jnp.int32, (per, lanes), 1)
        spread = jnp.broadcast_to(summed, (per, lanes))
        line = jnp.sum(
            jnp.where(2 * rows + side == cols, spread, 0.0), axis=0, keepdims=True
        )
        share[...] = line
        landing[side * shards + shard] = line
        each_other(lambda copy: copy.start())

    @pl.when(pair > 0)
    def _():
        for copy in small_copies(side):
            copy.wait_send()
        def settle(turn, part, which):
            for copy in (to_partner, to_across, to_beside, to_beside_again):
                copy(turn, part, which).wait_send()

        for_parts(settle)

    @pl.when(pair == last)
    def _():
        each_other(lambda copy: copy.wait_send())

    for origin in range(2 * shards):
        aa, ba = 2 * last + origin // shards, origin % shards

        @pl.when(jnp.logical_or(section != aa, shard != ba))
        def _():
            heard(aa, ba, origin)

    result = landing[0]
    for origin in range(1, 2 * shards):
        result = result + landing[origin]
    out[...] = result


def solution(mesh):
    sections, shards = mesh.shape["aa"], mesh.shape["ba"]

    def local(
        patches,
        token_first,
        token_second,
        channel_first,
        channel_second,
        gains,
        final_gain,
        head_weight,
        depths,
        widths,
        labels,
    ):
        images, patch_count, model = patches.shape
        candidates = depths.shape[0]
        slots = candidates // 2 * images
        group = 2 if slots % 2 == 0 else 1
        lanes = pl.cdiv(candidates, 128) * 128
        vmem = pl.BlockSpec(memory_space=pltpu.VMEM)
        hbm = pl.BlockSpec(memory_space=pltpu.HBM)
        bf16 = jnp.bfloat16
        dma = pltpu.SemaphoreType.DMA
        line = pl.pallas_call(
            functools.partial(kernel, sections, shards),
            out_shape=jax.ShapeDtypeStruct((1, lanes), jnp.float32),
            in_specs=[hbm] * 11,
            out_specs=vmem,
            scratch_shapes=[
                pltpu.SMEM(depths.shape[::-1], jnp.int32),
                pltpu.SMEM(widths.shape[::-1], jnp.int32),
                pltpu.SMEM(labels.shape, jnp.int32),
                pltpu.VMEM(patches.shape, bf16),
                pltpu.VMEM((1, model), jnp.float32),
                pltpu.VMEM((slots, patch_count, model), bf16),
                pltpu.VMEM((2 * slots, patch_count, model), bf16),
                pltpu.VMEM(((QUARTERS + 1) * QUARTERS, patch_count, model), bf16),
                pltpu.VMEM((2,) + token_first.shape[1:], bf16),
                pltpu.VMEM((2,) + token_second.shape[1:], bf16),
                pltpu.VMEM(
                    (2, group * token_first.shape[2], group * patch_count), bf16
                ),
                pltpu.VMEM((2,) + channel_first.shape[1:], bf16),
                pltpu.VMEM((2,) + channel_second.shape[1:], bf16),
                pltpu.VMEM((2,) + gains.shape[1:], jnp.float32),
                pltpu.VMEM(head_weight.shape[::-1], bf16),
                pltpu.VMEM((slots + 8, model), jnp.float32),
                pltpu.VMEM((1, lanes), jnp.float32),
                pltpu.VMEM((2 * shards, 1, lanes), jnp.float32),
                dma((11,)),
                dma((3,)),
                dma((3,)),
                dma((4, QUARTERS, PARTS, 2)),
                dma((TEAM, QUARTERS, PARTS, 2)),
                dma((2 * slots,)),
                dma((slots,)),
                dma((sections * shards,)),
                dma((2 * shards,)),
                pltpu.SemaphoreType.REGULAR,
            ],
            compiler_params=pltpu.CompilerParams(
                collective_id=0,
                has_side_effects=True,
                vmem_limit_bytes=58 * 1024 * 1024,
            ),
        )(
            depths.T,
            widths.T,
            labels,
            patches,
            gains,
            token_first,
            token_second,
            channel_first,
            channel_second,
            final_gain[None, :],
            head_weight.T,
        )
        return line[0, :candidates]

    return jax.shard_map(
        local,
        mesh=mesh,
        in_specs=(
            P("ba", None, None),
            P("aa", None, None),
            P("aa", None, None),
            P("aa", None, None),
            P("aa", None, None),
            P("aa", None, None),
            P(),
            P(),
            P(),
            P(),
            P("ba"),
        ),
        out_specs=P(),
        check_vma=False,
    )
```

```python
import functools

import jax
import jax.numpy as jnp
from jax import lax
from jax.experimental import pallas as pl
from jax.experimental.pallas import tpu as pltpu
from jax.sharding import PartitionSpec as P

UNIT = 4
QUARTERS = 4
TEAM = 4
PARTS = 2
LAG = 2
AHEAD = 8
MESH = pl.DeviceIdType.MESH
GELU_A = 0.7978845608028654
GELU_B = 0.044715 * GELU_A


def layer_norm(values, gain):
    center = values - jnp.mean(values, axis=-1, keepdims=True)
    spread = jnp.mean(center * center, axis=-1, keepdims=True)
    return center * lax.rsqrt(spread + 1e-06) * gain


def quick_norm(values, gain, pivot=None):
    if pivot is not None:
        values = values - pivot
    mean = jnp.mean(values, axis=-1, keepdims=True)
    square = jnp.mean(values * values, axis=-1, keepdims=True)
    spread = jnp.maximum(square - mean * mean, 0.0)
    return (values - mean) * lax.rsqrt(spread + 1e-06) * gain, mean


def gelu(x, half):
    x = x.astype(jnp.bfloat16)
    bent = jnp.tanh(x * (jnp.bfloat16(GELU_A) + jnp.bfloat16(GELU_B) * (x * x)))
    scaled = x * half
    return scaled + scaled * bent


def dot(a, b):
    return jnp.dot(a, b, preferred_element_type=jnp.float32)


def token_mix(floats, gain, token_one_t, token_two, quick=False):
    model = floats[0].shape[1]
    if quick:
        pairs = [quick_norm(value, gain) for value in floats]
        normed = [norm for norm, _ in pairs]
        means = jnp.concatenate([mean for _, mean in pairs], axis=0)
    else:
        normed = [layer_norm(value, gain) for value in floats]
        means = None
    normed = jnp.concatenate([norm.astype(jnp.bfloat16) for norm in normed], axis=1)
    hidden = gelu(dot(token_one_t, normed), jnp.bfloat16(0.5))
    part = dot(token_two, hidden)
    mixed = jnp.concatenate(
        [
            value + part[:, unit * model : (unit + 1) * model]
            for unit, value in enumerate(floats)
        ],
        axis=0,
    )
    return (mixed, means) if quick else mixed


def token_mix_rows(rows, units, gain, token_one_wide, token_two):
    normed, means = quick_norm(rows, gain)
    hidden = gelu(dot(token_one_wide, normed.astype(jnp.bfloat16)), jnp.bfloat16(0.5))
    height = hidden.shape[0] // units
    part = [
        dot(token_two, hidden[unit * height : (unit + 1) * height])
        for unit in range(units)
    ]
    return rows + jnp.concatenate(part, axis=0), means


def diagonal(block, count):
    zero = jnp.zeros_like(block)
    return jnp.concatenate(
        [
            jnp.concatenate(
                [block if row == column else zero for column in range(count)], axis=1
            )
            for row in range(count)
        ],
        axis=0,
    )


def kernel(
    sections,
    shards,
    depths_in,
    widths_in,
    labels_in,
    patches_in,
    gains,
    token_first,
    token_second,
    channel_first,
    channel_second,
    final_gain_in,
    head_weight_t,
    out,
    depths,
    widths,
    labels,
    patches,
    final_gain,
    inbox,
    outbox,
    options,
    token_one,
    token_two,
    token_one_t,
    channel_one,
    channel_two,
    gain_pair,
    head,
    pooled,
    share,
    landing,
    load_sem,
    small_send,
    small_recv,
    weight_send,
    weight_recv,
    state_send,
    state_recv,
    share_send,
    landing_sem,
    turn_sem,
):
    section = lax.axis_index("aa")
    shard = lax.axis_index("ba")
    pair = section // 2
    side = section % 2
    pairs = sections // 2
    last = pairs - 1
    images, patch_count, model = patches_in.shape
    candidates = depths_in.shape[1]
    per = candidates // 2
    slots = per * images
    hidden_units = channel_first.shape[2]
    quarter = hidden_units // QUARTERS
    partner = section + 1 - 2 * side
    rank = shard % TEAM
    team = shard - rank
    beside = team + rank + 1 - 2 * (rank % 2)
    across = team + (rank + 2) % TEAM

    loads = [
        pltpu.make_async_copy(source.at[0], target.at[side], load_sem.at[index])
        for index, (source, target) in enumerate(
            (
                (token_first, token_one),
                (token_second, token_two),
                (channel_first, channel_one),
                (channel_second, channel_two),
                (gains, gain_pair),
            )
        )
    ]
    head_load = pltpu.make_async_copy(head_weight_t, head, load_sem.at[5])
    tables = [
        pltpu.make_async_copy(source, target, load_sem.at[6 + index])
        for index, (source, target) in enumerate(
            (
                (patches_in, patches),
                (depths_in, depths),
                (widths_in, widths),
                (labels_in, labels),
                (final_gain_in, final_gain),
            )
        )
    ]
    loads = loads + tables
    barrier = pltpu.get_barrier_semaphore()

    def greet(aa, ba):
        pl.semaphore_signal(barrier, inc=1, device_id=(aa, ba), device_id_type=MESH)

    @pl.when(pair == 0)
    def _():
        greet(partner, shard)

    @pl.when(pair == 1)
    def _():
        greet(side, shard)

    @pl.when(pair > 0)
    def _():
        greet(partner, shard)
        greet(section, beside)
        greet(section, across)

    @pl.when(pair > 1)
    def _():
        greet(section - 2, shard)

    for load in loads:
        load.start()

    @pl.when(pair == last)
    def _():
        head_load.start()

    def greet_last(target, carry):
        aa, ba = 2 * last + target // shards, target % shards

        @pl.when(jnp.logical_or(aa != section, ba != shard))
        def _():
            greet(aa, ba)

        return carry

    lax.fori_loop(0, 2 * shards, greet_last, 0)

    @pl.when(section == 1)
    def _():
        pl.semaphore_wait(barrier, 2)

    @pl.when(jnp.logical_and(pair > 0, pair < last))
    def _():
        pl.semaphore_wait(barrier, 4)

    @pl.when(pair == last)
    def _():
        pl.semaphore_wait(barrier, sections * shards + 2)

    def state_copy(source, target, aa):
        return pltpu.make_async_remote_copy(
            src_ref=outbox.at[source],
            dst_ref=inbox.at[target],
            send_sem=state_send.at[source],
            recv_sem=state_recv.at[target],
            device_id=(aa, shard),
            device_id_type=MESH,
        )

    def arrived(slot):
        state_copy(slot, slot, section).wait_recv()

    @pl.when(section == 0)
    def _():
        for load in loads:
            load.wait()
        floats = [patches[image].astype(jnp.float32) for image in range(images)]
        mixed = token_mix(floats, gain_pair[0, 0:1, :], token_one[0].T, token_two[0])
        second = layer_norm(mixed, gain_pair[0, 1:2, :]).astype(jnp.bfloat16)
        total = mixed
        for width in range(QUARTERS):
            cut = slice(width * quarter, (width + 1) * quarter)
            hidden = gelu(dot(second, channel_one[0, :, cut]), jnp.bfloat16(0.5))
            total = total + dot(hidden, channel_two[0, cut, :])
            rounded = total.astype(jnp.bfloat16)
            for image in range(images):
                slot = image * QUARTERS + width
                outbox[slot] = rounded[image * patch_count : (image + 1) * patch_count]
        pl.semaphore_wait(barrier, 2)
        for slot in range(images * QUARTERS):
            state_copy(slot, slot, 1).start()

        def relay(slot):
            return pltpu.make_async_remote_copy(
                src_ref=inbox.at[slot],
                dst_ref=inbox.at[slot],
                send_sem=state_send.at[slots + slot],
                recv_sem=state_recv.at[slot],
                device_id=(2, shard),
                device_id_type=MESH,
            )

        def pass_on(slot, carry):
            arrived(slot)
            relay(slot).start()
            return carry

        def drain(slot, carry):
            relay(slot).wait_send()
            return carry

        lax.fori_loop(0, slots, pass_on, 0)
        lax.fori_loop(0, slots, drain, 0)
        for slot in range(images * QUARTERS):
            state_copy(slot, slot, 1).wait_send()

    @pl.when(section == 1)
    def _():
        for load in loads:
            load.wait()

        def image_step(image, carry):
            base = image * QUARTERS
            for width in range(QUARTERS):
                arrived(base + width)
            states = [inbox[base + width] for width in range(QUARTERS)]
            floats = [state.astype(jnp.float32) for state in states]
            mixed = token_mix(
                floats, gain_pair[1, 0:1, :], token_one[1].T, token_two[1]
            )
            second = layer_norm(mixed, gain_pair[1, 1:2, :]).astype(jnp.bfloat16)
            total = mixed
            for first in range(QUARTERS):
                options[first] = states[first]
            for width in range(QUARTERS):
                cut = slice(width * quarter, (width + 1) * quarter)
                hidden = gelu(dot(second, channel_one[1, :, cut]), jnp.bfloat16(0.5))
                total = total + dot(hidden, channel_two[1, cut, :])
                rounded = total.astype(jnp.bfloat16)
                for first in range(QUARTERS):
                    options[(width + 1) * QUARTERS + first] = rounded[
                        first * patch_count : (first + 1) * patch_count
                    ]

            def pick(index, carry):
                for parity in range(2):
                    candidate = 2 * index + parity
                    active = 1 < depths[0, candidate]
                    chosen = jnp.where(active, widths[1, candidate], 0)
                    row = chosen * QUARTERS + jnp.maximum(widths[0, candidate], 1) - 1
                    slot = image * per + index
                    outbox[parity * slots + slot] = options[row]
                    state_copy(parity * slots + slot, slot, 3 * parity).start()
                return carry

            lax.fori_loop(0, per, pick, 0)
            return carry

        lax.fori_loop(0, images, image_step, 0)

        def drain(index, carry):
            state_copy(index, index % slots, 2).wait_send()
            return carry

        lax.fori_loop(0, 2 * slots, drain, 0)

    rounds = QUARTERS
    group = 2 if slots % 2 == 0 else 1

    def region(turn, owner, part):
        spans = []
        for height in (model, hidden_units):
            rows = height // (rounds * TEAM * PARTS)
            start = ((turn * TEAM + owner) * PARTS + part) * rows
            spans.append((pl.ds(pl.multiple_of(start, rows), rows), slice(None)))
        return spans

    def weight_copy(parity, from_input, kind, turn, part, owner, aa, ba, which):
        rows, columns = region(turn, owner, part)[which]
        target = (channel_one, channel_two)[which].at[parity, rows, columns]
        if from_input:
            ref = (channel_first, channel_second)[which].at[0, rows, columns]
        else:
            ref = target
        return pltpu.make_async_remote_copy(
            src_ref=ref,
            dst_ref=target,
            send_sem=weight_send.at[kind, turn, part, which],
            recv_sem=weight_recv.at[owner, turn, part, which],
            device_id=(aa, ba),
            device_id_type=MESH,
        )

    other = 1 - side

    def small_copies(part):
        return [
            pltpu.make_async_remote_copy(
                src_ref=source.at[0],
                dst_ref=target.at[part],
                send_sem=small_send.at[index],
                recv_sem=small_recv.at[index],
                device_id=(partner, shard),
                device_id_type=MESH,
            )
            for index, (source, target) in enumerate(
                (
                    (token_first, token_one),
                    (token_second, token_two),
                    (gains, gain_pair),
                )
            )
        ]

    rank_beside = rank + 1 - 2 * (rank % 2)
    rank_across = (rank + 2) % TEAM
    rank_far = (rank_beside + 2) % TEAM

    def to_partner(turn, part, which):
        return weight_copy(side, True, 0, turn, part, rank, partner, shard, which)

    def to_across(turn, part, which):
        return weight_copy(other, False, 1, turn, part, rank, section, across, which)

    def to_beside(turn, part, which):
        return weight_copy(other, False, 2, turn, part, rank, section, beside, which)

    def to_beside_again(turn, part, which):
        return weight_copy(
            other, False, 3, turn, part, rank_across, section, beside, which
        )

    def from_owner(turn, owner, part, which):
        return weight_copy(other, False, 0, turn, part, owner, section, shard, which)

    def for_parts(act):
        def visit(index, carry):
            for which in range(2):
                act(index // PARTS, index % PARTS, which)
            return carry

        lax.fori_loop(0, rounds * PARTS, visit, 0)

    def section_step(group, first, finish, parity, states):
        here = 2 * pair + parity
        mixed, means = token_mix_rows(
            jnp.concatenate(states, axis=0).astype(jnp.float32),
            group,
            gain_pair[parity, 0:1, :],
            token_one_t[parity],
            token_two[parity],
        )
        second, _ = quick_norm(mixed, gain_pair[parity, 1:2, :], means)
        second = second.astype(jnp.bfloat16)
        pre = dot(second, channel_one[parity])
        lane = lax.broadcasted_iota(jnp.int32, (1, hidden_units), 1)
        parts = []
        actives = []
        for unit in range(group):
            candidate = 2 * ((first + unit) % per) + side
            actives.append(here % UNIT < depths[here // UNIT, candidate])
            half = jnp.where(lane < widths[here, candidate] * quarter, 0.5, 0.0).astype(
                jnp.bfloat16
            )
            rows = slice(unit * patch_count, (unit + 1) * patch_count)
            parts.append(gelu(pre[rows], half))
        hidden = jnp.concatenate(parts, axis=0)
        total = (mixed + dot(hidden, channel_two[parity])).astype(jnp.bfloat16)
        return [
            jnp.where(
                actives[unit],
                total[unit * patch_count : (unit + 1) * patch_count],
                states[unit],
            )
            for unit in range(group)
        ]

    def pool(source, row):
        final = layer_norm(outbox[source].astype(jnp.float32), final_gain[...])
        pooled[pl.ds(row, 1), :] = jnp.mean(final, axis=0, keepdims=True)

    def chunk(group, finish, index, carry):
        first = index * group
        for unit in range(group):
            arrived(first + unit)

        def both(parity, carry):
            states = [inbox[first + unit] for unit in range(group)]
            updated = section_step(group, first, finish, parity, states)
            if finish:
                unit = jnp.minimum(parity, group - 1)
                row = jnp.where(index == 0, slots, first - group) + unit
                pool(row, row)
            for unit in range(group):
                outbox[first + unit] = updated[unit]

            @pl.when(parity == 0)
            def _():
                for unit in range(group):
                    inbox[first + unit] = updated[unit]

                @pl.when((pair == 1) & (index == 0) & (rank % 2 == 0))
                def _():
                    pl.semaphore_signal(
                        turn_sem,
                        inc=1,
                        device_id=(section, beside),
                        device_id_type=MESH,
                    )

            return carry

        lax.fori_loop(0, 2, both, 0)
        if not finish:
            for unit in range(group):
                state_copy(first + unit, first + unit, section + 2).start()
        return carry

    @pl.when(pair > 0)
    def _():
        for copy in small_copies(side):
            copy.start()
        for index in range(AHEAD):
            for which in range(2):
                to_partner(index // PARTS, index % PARTS, which).start()

        for load in loads:
            load.wait()
        token_one_t[side] = diagonal(token_one[side].T, group)
        for copy in small_copies(other):
            copy.wait_recv()
        token_one_t[other] = diagonal(token_one[other].T, group)
        def forward(turn, part, which):
            from_owner(turn, rank, part, which).wait_recv()
            to_across(turn, part, which).start()
            to_beside(turn, part, which).start()
            follow = turn * PARTS + part + AHEAD

            @pl.when(follow < rounds * PARTS)
            def _():
                to_partner(follow // PARTS, follow % PARTS, which).start()

            before = turn * PARTS + part - LAG
            if which == 1:

                @pl.when(before >= 0)
                def _():
                    forward_again(before)

        def forward_again(index):
            turn, part = index // PARTS, index % PARTS
            for which in range(2):
                from_owner(turn, rank_across, part, which).wait_recv()
                to_beside_again(turn, part, which).start()

        def finish(turn, part, which):
            from_owner(turn, rank_beside, part, which).wait_recv()
            from_owner(turn, rank_far, part, which).wait_recv()

        for_parts(forward)
        for index in range(rounds * PARTS - LAG, rounds * PARTS):
            forward_again(index)
        for_parts(finish)

        @pl.when((pair == 1) & (rank % 2 == 1))
        def _():
            pl.semaphore_wait(turn_sem, 1)

        steps = slots // group

        @pl.when(pair < last)
        def _():
            lax.fori_loop(0, steps, functools.partial(chunk, group, False), 0)

        @pl.when(pair == last)
        def _():
            for unit in range(group):
                outbox[slots + unit] = jnp.zeros((patch_count, model), jnp.bfloat16)
            lax.fori_loop(0, steps, functools.partial(chunk, group, True), 0)
            for unit in range(group):
                pool(slots - group + unit, slots - group + unit)

    @pl.when(jnp.logical_and(pair > 0, pair < last))
    def _():
        def drain(slot, carry):
            state_copy(slot, slot, section + 2).wait_send()
            return carry

        lax.fori_loop(0, slots, drain, 0)

    def tell(aa, ba):
        mine = side * shards + shard
        return pltpu.make_async_remote_copy(
            src_ref=share,
            dst_ref=landing.at[mine],
            send_sem=share_send.at[aa * shards + ba],
            recv_sem=landing_sem.at[mine],
            device_id=(aa, ba),
            device_id_type=MESH,
        )

    def each_other(act):
        def visit(target, carry):
            aa, ba = target // shards, target % shards

            @pl.when(jnp.logical_or(aa != section, ba != shard))
            def _():
                act(tell(aa, ba))

            return carry

        lax.fori_loop(0, sections * shards, visit, 0)

    def heard(aa, ba, origin):
        pltpu.make_async_remote_copy(
            src_ref=share,
            dst_ref=landing.at[origin],
            send_sem=share_send.at[0],
            recv_sem=landing_sem.at[origin],
            device_id=(aa, ba),
            device_id_type=MESH,
        ).wait_recv()

    @pl.when(pair == last)
    def _():
        head_load.wait()
        logits = lax.dot_general(
            pooled[:slots].astype(jnp.bfloat16),
            head[...],
            (((1,), (1,)), ((), ())),
            preferred_element_type=jnp.float32,
        )
        top = jnp.max(logits, axis=-1, keepdims=True)
        total = top + jnp.log(jnp.sum(jnp.exp(logits - top), axis=-1, keepdims=True))
        rows = lax.broadcasted_iota(jnp.int32, logits.shape, 0)
        classes = lax.broadcasted_iota(jnp.int32, logits.shape, 1)
        wanted = jnp.full(logits.shape, labels[0], jnp.int32)
        for image in range(1, images):
            wanted = jnp.where(rows >= image * per, labels[image], wanted)
        picked = jnp.sum(
            jnp.where(classes == wanted, logits, 0.0), axis=-1, keepdims=True
        )
        losses = total - picked
        summed = losses[:per]
        for image in range(1, images):
            summed = summed + losses[image * per : (image + 1) * per]
        lanes = out.shape[1]
        rows = lax.broadcasted_iota(jnp.int32, (per, lanes), 0)
        cols = lax.broadcasted_iota(jnp.int32, (per, lanes), 1)
        spread = jnp.broadcast_to(summed, (per, lanes))
        line = jnp.sum(
            jnp.where(2 * rows + side == cols, spread, 0.0), axis=0, keepdims=True
        )
        share[...] = line
        landing[side * shards + shard] = line
        each_other(lambda copy: copy.start())

    @pl.when(pair > 0)
    def _():
        for copy in small_copies(side):
            copy.wait_send()
        def settle(turn, part, which):
            for copy in (to_partner, to_across, to_beside, to_beside_again):
                copy(turn, part, which).wait_send()

        for_parts(settle)

    @pl.when(pair == last)
    def _():
        each_other(lambda copy: copy.wait_send())

    for origin in range(2 * shards):
        aa, ba = 2 * last + origin // shards, origin % shards

        @pl.when(jnp.logical_or(section != aa, shard != ba))
        def _():
            heard(aa, ba, origin)

    result = landing[0]
    for origin in range(1, 2 * shards):
        result = result + landing[origin]
    out[...] = result


def solution(mesh):
    sections, shards = mesh.shape["aa"], mesh.shape["ba"]

    def local(
        patches,
        token_first,
        token_second,
        channel_first,
        channel_second,
        gains,
        final_gain,
        head_weight,
        depths,
        widths,
        labels,
    ):
        images, patch_count, model = patches.shape
        candidates = depths.shape[0]
        slots = candidates // 2 * images
        group = 2 if slots % 2 == 0 else 1
        lanes = pl.cdiv(candidates, 128) * 128
        vmem = pl.BlockSpec(memory_space=pltpu.VMEM)
        hbm = pl.BlockSpec(memory_space=pltpu.HBM)
        bf16 = jnp.bfloat16
        dma = pltpu.SemaphoreType.DMA
        line = pl.pallas_call(
            functools.partial(kernel, sections, shards),
            out_shape=jax.ShapeDtypeStruct((1, lanes), jnp.float32),
            in_specs=[hbm] * 11,
            out_specs=vmem,
            scratch_shapes=[
                pltpu.SMEM(depths.shape[::-1], jnp.int32),
                pltpu.SMEM(widths.shape[::-1], jnp.int32),
                pltpu.SMEM(labels.shape, jnp.int32),
                pltpu.VMEM(patches.shape, bf16),
                pltpu.VMEM((1, model), jnp.float32),
                pltpu.VMEM((slots, patch_count, model), bf16),
                pltpu.VMEM((2 * slots, patch_count, model), bf16),
                pltpu.VMEM(((QUARTERS + 1) * QUARTERS, patch_count, model), bf16),
                pltpu.VMEM((2,) + token_first.shape[1:], bf16),
                pltpu.VMEM((2,) + token_second.shape[1:], bf16),
                pltpu.VMEM(
                    (2, group * token_first.shape[2], group * patch_count), bf16
                ),
                pltpu.VMEM((2,) + channel_first.shape[1:], bf16),
                pltpu.VMEM((2,) + channel_second.shape[1:], bf16),
                pltpu.VMEM((2,) + gains.shape[1:], jnp.float32),
                pltpu.VMEM(head_weight.shape[::-1], bf16),
                pltpu.VMEM((slots + 8, model), jnp.float32),
                pltpu.VMEM((1, lanes), jnp.float32),
                pltpu.VMEM((2 * shards, 1, lanes), jnp.float32),
                dma((11,)),
                dma((3,)),
                dma((3,)),
                dma((4, QUARTERS, PARTS, 2)),
                dma((TEAM, QUARTERS, PARTS, 2)),
                dma((2 * slots,)),
                dma((slots,)),
                dma((sections * shards,)),
                dma((2 * shards,)),
                pltpu.SemaphoreType.REGULAR,
            ],
            compiler_params=pltpu.CompilerParams(
                collective_id=0,
                has_side_effects=True,
                vmem_limit_bytes=58 * 1024 * 1024,
            ),
        )(
            depths.T,
            widths.T,
            labels,
            patches,
            gains,
            token_first,
            token_second,
            channel_first,
            channel_second,
            final_gain[None, :],
            head_weight.T,
        )
        return line[0, :candidates]

    return jax.shard_map(
        local,
        mesh=mesh,
        in_specs=(
            P("ba", None, None),
            P("aa", None, None),
            P("aa", None, None),
            P("aa", None, None),
            P("aa", None, None),
            P("aa", None, None),
            P(),
            P(),
            P(),
            P(),
            P("ba"),
        ),
        out_specs=P(),
        check_vma=False,
    )
```

```python
import functools

import jax
import jax.numpy as jnp
from jax import lax
from jax.experimental import pallas as pl
from jax.experimental.pallas import tpu as pltpu
from jax.sharding import PartitionSpec as P

UNIT = 4
QUARTERS = 4
TEAM = 4
PARTS = 2
LAG = 1
AHEAD = 2
MESH = pl.DeviceIdType.MESH
GELU_A = 0.7978845608028654
GELU_B = 0.044715 * GELU_A


def layer_norm(values, gain):
    center = values - jnp.mean(values, axis=-1, keepdims=True)
    spread = jnp.mean(center * center, axis=-1, keepdims=True)
    return center * lax.rsqrt(spread + 1e-06) * gain


def quick_norm(values, gain, pivot=None):
    if pivot is not None:
        values = values - pivot
    mean = jnp.mean(values, axis=-1, keepdims=True)
    square = jnp.mean(values * values, axis=-1, keepdims=True)
    spread = jnp.maximum(square - mean * mean, 0.0)
    return (values - mean) * lax.rsqrt(spread + 1e-06) * gain, mean


def gelu(x, half):
    x = x.astype(jnp.bfloat16)
    bent = jnp.tanh(x * (jnp.bfloat16(GELU_A) + jnp.bfloat16(GELU_B) * (x * x)))
    scaled = x * half
    return scaled + scaled * bent


def dot(a, b):
    return jnp.dot(a, b, preferred_element_type=jnp.float32)


def token_mix(floats, gain, token_one_t, token_two, quick=False):
    model = floats[0].shape[1]
    if quick:
        pairs = [quick_norm(value, gain) for value in floats]
        normed = [norm for norm, _ in pairs]
        means = jnp.concatenate([mean for _, mean in pairs], axis=0)
    else:
        normed = [layer_norm(value, gain) for value in floats]
        means = None
    normed = jnp.concatenate([norm.astype(jnp.bfloat16) for norm in normed], axis=1)
    hidden = gelu(dot(token_one_t, normed), jnp.bfloat16(0.5))
    part = dot(token_two, hidden)
    mixed = jnp.concatenate(
        [
            value + part[:, unit * model : (unit + 1) * model]
            for unit, value in enumerate(floats)
        ],
        axis=0,
    )
    return (mixed, means) if quick else mixed


def token_mix_rows(rows, units, gain, token_one_wide, token_two):
    normed, means = quick_norm(rows, gain)
    hidden = gelu(dot(token_one_wide, normed.astype(jnp.bfloat16)), jnp.bfloat16(0.5))
    height = hidden.shape[0] // units
    part = [
        dot(token_two, hidden[unit * height : (unit + 1) * height])
        for unit in range(units)
    ]
    return rows + jnp.concatenate(part, axis=0), means


def diagonal(block, count):
    zero = jnp.zeros_like(block)
    return jnp.concatenate(
        [
            jnp.concatenate(
                [block if row == column else zero for column in range(count)], axis=1
            )
            for row in range(count)
        ],
        axis=0,
    )


def kernel(
    sections,
    shards,
    depths_in,
    widths_in,
    labels_in,
    patches_in,
    gains,
    token_first,
    token_second,
    channel_first,
    channel_second,
    final_gain_in,
    head_weight_t,
    out,
    depths,
    widths,
    labels,
    patches,
    final_gain,
    inbox,
    outbox,
    options,
    token_one,
    token_two,
    token_one_t,
    channel_one,
    channel_two,
    gain_pair,
    head,
    pooled,
    share,
    landing,
    load_sem,
    small_send,
    small_recv,
    weight_send,
    weight_recv,
    state_send,
    state_recv,
    share_send,
    landing_sem,
    turn_sem,
):
    section = lax.axis_index("aa")
    shard = lax.axis_index("ba")
    pair = section // 2
    side = section % 2
    pairs = sections // 2
    last = pairs - 1
    images, patch_count, model = patches_in.shape
    candidates = depths_in.shape[1]
    per = candidates // 2
    slots = per * images
    hidden_units = channel_first.shape[2]
    quarter = hidden_units // QUARTERS
    partner = section + 1 - 2 * side
    rank = shard % TEAM
    team = shard - rank
    beside = team + rank + 1 - 2 * (rank % 2)
    across = team + (rank + 2) % TEAM

    loads = [
        pltpu.make_async_copy(source.at[0], target.at[side], load_sem.at[index])
        for index, (source, target) in enumerate(
            (
                (token_first, token_one),
                (token_second, token_two),
                (channel_first, channel_one),
                (channel_second, channel_two),
                (gains, gain_pair),
            )
        )
    ]
    head_load = pltpu.make_async_copy(head_weight_t, head, load_sem.at[5])
    tables = [
        pltpu.make_async_copy(source, target, load_sem.at[6 + index])
        for index, (source, target) in enumerate(
            (
                (patches_in, patches),
                (depths_in, depths),
                (widths_in, widths),
                (labels_in, labels),
                (final_gain_in, final_gain),
            )
        )
    ]
    loads = loads + tables
    barrier = pltpu.get_barrier_semaphore()

    def greet(aa, ba):
        pl.semaphore_signal(barrier, inc=1, device_id=(aa, ba), device_id_type=MESH)

    @pl.when(pair == 0)
    def _():
        greet(partner, shard)

    @pl.when(pair == 1)
    def _():
        greet(side, shard)

    @pl.when(pair > 0)
    def _():
        greet(partner, shard)
        greet(section, beside)
        greet(section, across)

    @pl.when(pair > 1)
    def _():
        greet(section - 2, shard)

    for load in loads:
        load.start()

    @pl.when(pair == last)
    def _():
        head_load.start()

    def greet_last(target, carry):
        aa, ba = 2 * last + target // shards, target % shards

        @pl.when(jnp.logical_or(aa != section, ba != shard))
        def _():
            greet(aa, ba)

        return carry

    lax.fori_loop(0, 2 * shards, greet_last, 0)

    @pl.when(section == 1)
    def _():
        pl.semaphore_wait(barrier, 2)

    @pl.when(jnp.logical_and(pair > 0, pair < last))
    def _():
        pl.semaphore_wait(barrier, 4)

    @pl.when(pair == last)
    def _():
        pl.semaphore_wait(barrier, sections * shards + 2)

    def state_copy(source, target, aa):
        return pltpu.make_async_remote_copy(
            src_ref=outbox.at[source],
            dst_ref=inbox.at[target],
            send_sem=state_send.at[source],
            recv_sem=state_recv.at[target],
            device_id=(aa, shard),
            device_id_type=MESH,
        )

    def arrived(slot):
        state_copy(slot, slot, section).wait_recv()

    @pl.when(section == 0)
    def _():
        for load in loads:
            load.wait()
        floats = [patches[image].astype(jnp.float32) for image in range(images)]
        mixed = token_mix(floats, gain_pair[0, 0:1, :], token_one[0].T, token_two[0])
        second = layer_norm(mixed, gain_pair[0, 1:2, :]).astype(jnp.bfloat16)
        total = mixed
        for width in range(QUARTERS):
            cut = slice(width * quarter, (width + 1) * quarter)
            hidden = gelu(dot(second, channel_one[0, :, cut]), jnp.bfloat16(0.5))
            total = total + dot(hidden, channel_two[0, cut, :])
            rounded = total.astype(jnp.bfloat16)
            for image in range(images):
                slot = image * QUARTERS + width
                outbox[slot] = rounded[image * patch_count : (image + 1) * patch_count]
        pl.semaphore_wait(barrier, 2)
        for slot in range(images * QUARTERS):
            state_copy(slot, slot, 1).start()

        def relay(slot):
            return pltpu.make_async_remote_copy(
                src_ref=inbox.at[slot],
                dst_ref=inbox.at[slot],
                send_sem=state_send.at[slots + slot],
                recv_sem=state_recv.at[slot],
                device_id=(2, shard),
                device_id_type=MESH,
            )

        def pass_on(slot, carry):
            arrived(slot)
            relay(slot).start()
            return carry

        def drain(slot, carry):
            relay(slot).wait_send()
            return carry

        lax.fori_loop(0, slots, pass_on, 0)
        lax.fori_loop(0, slots, drain, 0)
        for slot in range(images * QUARTERS):
            state_copy(slot, slot, 1).wait_send()

    @pl.when(section == 1)
    def _():
        for load in loads:
            load.wait()

        def image_step(image, carry):
            base = image * QUARTERS
            for width in range(QUARTERS):
                arrived(base + width)
            states = [inbox[base + width] for width in range(QUARTERS)]
            floats = [state.astype(jnp.float32) for state in states]
            mixed = token_mix(
                floats, gain_pair[1, 0:1, :], token_one[1].T, token_two[1]
            )
            second = layer_norm(mixed, gain_pair[1, 1:2, :]).astype(jnp.bfloat16)
            total = mixed
            for first in range(QUARTERS):
                options[first] = states[first]
            for width in range(QUARTERS):
                cut = slice(width * quarter, (width + 1) * quarter)
                hidden = gelu(dot(second, channel_one[1, :, cut]), jnp.bfloat16(0.5))
                total = total + dot(hidden, channel_two[1, cut, :])
                rounded = total.astype(jnp.bfloat16)
                for first in range(QUARTERS):
                    options[(width + 1) * QUARTERS + first] = rounded[
                        first * patch_count : (first + 1) * patch_count
                    ]

            def pick(index, carry):
                for parity in range(2):
                    candidate = 2 * index + parity
                    active = 1 < depths[0, candidate]
                    chosen = jnp.where(active, widths[1, candidate], 0)
                    row = chosen * QUARTERS + jnp.maximum(widths[0, candidate], 1) - 1
                    slot = image * per + index
                    outbox[parity * slots + slot] = options[row]
                    state_copy(parity * slots + slot, slot, 3 * parity).start()
                return carry

            lax.fori_loop(0, per, pick, 0)
            return carry

        lax.fori_loop(0, images, image_step, 0)

        def drain(index, carry):
            state_copy(index, index % slots, 2).wait_send()
            return carry

        lax.fori_loop(0, 2 * slots, drain, 0)

    rounds = QUARTERS
    group = 2 if slots % 2 == 0 else 1

    def region(turn, owner, part):
        spans = []
        for height in (model, hidden_units):
            rows = height // (rounds * TEAM * PARTS)
            start = ((turn * TEAM + owner) * PARTS + part) * rows
            spans.append((pl.ds(pl.multiple_of(start, rows), rows), slice(None)))
        return spans

    def weight_copy(parity, from_input, kind, turn, part, owner, aa, ba, which):
        rows, columns = region(turn, owner, part)[which]
        target = (channel_one, channel_two)[which].at[parity, rows, columns]
        if from_input:
            ref = (channel_first, channel_second)[which].at[0, rows, columns]
        else:
            ref = target
        return pltpu.make_async_remote_copy(
            src_ref=ref,
            dst_ref=target,
            send_sem=weight_send.at[kind, turn, part, which],
            recv_sem=weight_recv.at[owner, turn, part, which],
            device_id=(aa, ba),
            device_id_type=MESH,
        )

    other = 1 - side

    def small_copies(part):
        return [
            pltpu.make_async_remote_copy(
                src_ref=source.at[0],
                dst_ref=target.at[part],
                send_sem=small_send.at[index],
                recv_sem=small_recv.at[index],
                device_id=(partner, shard),
                device_id_type=MESH,
            )
            for index, (source, target) in enumerate(
                (
                    (token_first, token_one),
                    (token_second, token_two),
                    (gains, gain_pair),
                )
            )
        ]

    rank_beside = rank + 1 - 2 * (rank % 2)
    rank_across = (rank + 2) % TEAM
    rank_far = (rank_beside + 2) % TEAM

    def to_partner(turn, part, which):
        return weight_copy(side, True, 0, turn, part, rank, partner, shard, which)

    def to_across(turn, part, which):
        return weight_copy(other, False, 1, turn, part, rank, section, across, which)

    def to_beside(turn, part, which):
        return weight_copy(other, False, 2, turn, part, rank, section, beside, which)

    def to_beside_again(turn, part, which):
        return weight_copy(
            other, False, 3, turn, part, rank_across, section, beside, which
        )

    def from_owner(turn, owner, part, which):
        return weight_copy(other, False, 0, turn, part, owner, section, shard, which)

    def for_parts(act):
        def visit(index, carry):
            for which in range(2):
                act(index // PARTS, index % PARTS, which)
            return carry

        lax.fori_loop(0, rounds * PARTS, visit, 0)

    def section_step(group, first, finish, parity, states):
        here = 2 * pair + parity
        mixed, means = token_mix_rows(
            jnp.concatenate(states, axis=0).astype(jnp.float32),
            group,
            gain_pair[parity, 0:1, :],
            token_one_t[parity],
            token_two[parity],
        )
        second, _ = quick_norm(mixed, gain_pair[parity, 1:2, :], means)
        second = second.astype(jnp.bfloat16)
        pre = dot(second, channel_one[parity])
        lane = lax.broadcasted_iota(jnp.int32, (1, hidden_units), 1)
        parts = []
        actives = []
        for unit in range(group):
            candidate = 2 * ((first + unit) % per) + side
            actives.append(here % UNIT < depths[here // UNIT, candidate])
            half = jnp.where(lane < widths[here, candidate] * quarter, 0.5, 0.0).astype(
                jnp.bfloat16
            )
            rows = slice(unit * patch_count, (unit + 1) * patch_count)
            parts.append(gelu(pre[rows], half))
        hidden = jnp.concatenate(parts, axis=0)
        total = (mixed + dot(hidden, channel_two[parity])).astype(jnp.bfloat16)
        return [
            jnp.where(
                actives[unit],
                total[unit * patch_count : (unit + 1) * patch_count],
                states[unit],
            )
            for unit in range(group)
        ]

    def pool(source, row):
        final = layer_norm(outbox[source].astype(jnp.float32), final_gain[...])
        pooled[pl.ds(row, 1), :] = jnp.mean(final, axis=0, keepdims=True)

    def chunk(group, finish, index, carry):
        first = index * group
        for unit in range(group):
            arrived(first + unit)

        def both(parity, carry):
            states = [inbox[first + unit] for unit in range(group)]
            updated = section_step(group, first, finish, parity, states)
            if finish:
                unit = jnp.minimum(parity, group - 1)
                row = jnp.where(index == 0, slots, first - group) + unit
                pool(row, row)
            for unit in range(group):
                outbox[first + unit] = updated[unit]

            @pl.when(parity == 0)
            def _():
                for unit in range(group):
                    inbox[first + unit] = updated[unit]

                @pl.when((pair == 1) & (index == 0) & (rank % 2 == 0))
                def _():
                    pl.semaphore_signal(
                        turn_sem,
                        inc=1,
                        device_id=(section, beside),
                        device_id_type=MESH,
                    )

            return carry

        lax.fori_loop(0, 2, both, 0)
        if not finish:
            for unit in range(group):
                state_copy(first + unit, first + unit, section + 2).start()
        return carry

    @pl.when(pair > 0)
    def _():
        for copy in small_copies(side):
            copy.start()
        for index in range(AHEAD):
            for which in range(2):
                to_partner(index // PARTS, index % PARTS, which).start()

        for load in loads:
            load.wait()
        token_one_t[side] = diagonal(token_one[side].T, group)
        for copy in small_copies(other):
            copy.wait_recv()
        token_one_t[other] = diagonal(token_one[other].T, group)
        def forward(turn, part, which):
            from_owner(turn, rank, part, which).wait_recv()
            to_across(turn, part, which).start()
            to_beside(turn, part, which).start()
            follow = turn * PARTS + part + AHEAD

            @pl.when(follow < rounds * PARTS)
            def _():
                to_partner(follow // PARTS, follow % PARTS, which).start()

            before = turn * PARTS + part - LAG
            if which == 1:

                @pl.when(before >= 0)
                def _():
                    forward_again(before)

        def forward_again(index):
            turn, part = index // PARTS, index % PARTS
            for which in range(2):
                from_owner(turn, rank_across, part, which).wait_recv()
                to_beside_again(turn, part, which).start()

        def finish(turn, part, which):
            from_owner(turn, rank_beside, part, which).wait_recv()
            from_owner(turn, rank_far, part, which).wait_recv()

        for_parts(forward)
        for index in range(rounds * PARTS - LAG, rounds * PARTS):
            forward_again(index)
        for_parts(finish)

        @pl.when((pair == 1) & (rank % 2 == 1))
        def _():
            pl.semaphore_wait(turn_sem, 1)

        steps = slots // group

        @pl.when(pair < last)
        def _():
            lax.fori_loop(0, steps, functools.partial(chunk, group, False), 0)

        @pl.when(pair == last)
        def _():
            for unit in range(group):
                outbox[slots + unit] = jnp.zeros((patch_count, model), jnp.bfloat16)
            lax.fori_loop(0, steps, functools.partial(chunk, group, True), 0)
            for unit in range(group):
                pool(slots - group + unit, slots - group + unit)

    @pl.when(jnp.logical_and(pair > 0, pair < last))
    def _():
        def drain(slot, carry):
            state_copy(slot, slot, section + 2).wait_send()
            return carry

        lax.fori_loop(0, slots, drain, 0)

    def tell(aa, ba):
        mine = side * shards + shard
        return pltpu.make_async_remote_copy(
            src_ref=share,
            dst_ref=landing.at[mine],
            send_sem=share_send.at[aa * shards + ba],
            recv_sem=landing_sem.at[mine],
            device_id=(aa, ba),
            device_id_type=MESH,
        )

    def each_other(act):
        def visit(target, carry):
            aa, ba = target // shards, target % shards

            @pl.when(jnp.logical_or(aa != section, ba != shard))
            def _():
                act(tell(aa, ba))

            return carry

        lax.fori_loop(0, sections * shards, visit, 0)

    def heard(aa, ba, origin):
        pltpu.make_async_remote_copy(
            src_ref=share,
            dst_ref=landing.at[origin],
            send_sem=share_send.at[0],
            recv_sem=landing_sem.at[origin],
            device_id=(aa, ba),
            device_id_type=MESH,
        ).wait_recv()

    @pl.when(pair == last)
    def _():
        head_load.wait()
        logits = lax.dot_general(
            pooled[:slots].astype(jnp.bfloat16),
            head[...],
            (((1,), (1,)), ((), ())),
            preferred_element_type=jnp.float32,
        )
        top = jnp.max(logits, axis=-1, keepdims=True)
        total = top + jnp.log(jnp.sum(jnp.exp(logits - top), axis=-1, keepdims=True))
        rows = lax.broadcasted_iota(jnp.int32, logits.shape, 0)
        classes = lax.broadcasted_iota(jnp.int32, logits.shape, 1)
        wanted = jnp.full(logits.shape, labels[0], jnp.int32)
        for image in range(1, images):
            wanted = jnp.where(rows >= image * per, labels[image], wanted)
        picked = jnp.sum(
            jnp.where(classes == wanted, logits, 0.0), axis=-1, keepdims=True
        )
        losses = total - picked
        summed = losses[:per]
        for image in range(1, images):
            summed = summed + losses[image * per : (image + 1) * per]
        lanes = out.shape[1]
        rows = lax.broadcasted_iota(jnp.int32, (per, lanes), 0)
        cols = lax.broadcasted_iota(jnp.int32, (per, lanes), 1)
        spread = jnp.broadcast_to(summed, (per, lanes))
        line = jnp.sum(
            jnp.where(2 * rows + side == cols, spread, 0.0), axis=0, keepdims=True
        )
        share[...] = line
        landing[side * shards + shard] = line
        each_other(lambda copy: copy.start())

    @pl.when(pair > 0)
    def _():
        for copy in small_copies(side):
            copy.wait_send()
        def settle(turn, part, which):
            for copy in (to_partner, to_across, to_beside, to_beside_again):
                copy(turn, part, which).wait_send()

        for_parts(settle)

    @pl.when(pair == last)
    def _():
        each_other(lambda copy: copy.wait_send())

    for origin in range(2 * shards):
        aa, ba = 2 * last + origin // shards, origin % shards

        @pl.when(jnp.logical_or(section != aa, shard != ba))
        def _():
            heard(aa, ba, origin)

    result = landing[0]
    for origin in range(1, 2 * shards):
        result = result + landing[origin]
    out[...] = result


def solution(mesh):
    sections, shards = mesh.shape["aa"], mesh.shape["ba"]

    def local(
        patches,
        token_first,
        token_second,
        channel_first,
        channel_second,
        gains,
        final_gain,
        head_weight,
        depths,
        widths,
        labels,
    ):
        images, patch_count, model = patches.shape
        candidates = depths.shape[0]
        slots = candidates // 2 * images
        group = 2 if slots % 2 == 0 else 1
        lanes = pl.cdiv(candidates, 128) * 128
        vmem = pl.BlockSpec(memory_space=pltpu.VMEM)
        hbm = pl.BlockSpec(memory_space=pltpu.HBM)
        bf16 = jnp.bfloat16
        dma = pltpu.SemaphoreType.DMA
        line = pl.pallas_call(
            functools.partial(kernel, sections, shards),
            out_shape=jax.ShapeDtypeStruct((1, lanes), jnp.float32),
            in_specs=[hbm] * 11,
            out_specs=vmem,
            scratch_shapes=[
                pltpu.SMEM(depths.shape[::-1], jnp.int32),
                pltpu.SMEM(widths.shape[::-1], jnp.int32),
                pltpu.SMEM(labels.shape, jnp.int32),
                pltpu.VMEM(patches.shape, bf16),
                pltpu.VMEM((1, model), jnp.float32),
                pltpu.VMEM((slots, patch_count, model), bf16),
                pltpu.VMEM((2 * slots, patch_count, model), bf16),
                pltpu.VMEM(((QUARTERS + 1) * QUARTERS, patch_count, model), bf16),
                pltpu.VMEM((2,) + token_first.shape[1:], bf16),
                pltpu.VMEM((2,) + token_second.shape[1:], bf16),
                pltpu.VMEM(
                    (2, group * token_first.shape[2], group * patch_count), bf16
                ),
                pltpu.VMEM((2,) + channel_first.shape[1:], bf16),
                pltpu.VMEM((2,) + channel_second.shape[1:], bf16),
                pltpu.VMEM((2,) + gains.shape[1:], jnp.float32),
                pltpu.VMEM(head_weight.shape[::-1], bf16),
                pltpu.VMEM((slots + 8, model), jnp.float32),
                pltpu.VMEM((1, lanes), jnp.float32),
                pltpu.VMEM((2 * shards, 1, lanes), jnp.float32),
                dma((11,)),
                dma((3,)),
                dma((3,)),
                dma((4, QUARTERS, PARTS, 2)),
                dma((TEAM, QUARTERS, PARTS, 2)),
                dma((2 * slots,)),
                dma((slots,)),
                dma((sections * shards,)),
                dma((2 * shards,)),
                pltpu.SemaphoreType.REGULAR,
            ],
            compiler_params=pltpu.CompilerParams(
                collective_id=0,
                has_side_effects=True,
                vmem_limit_bytes=58 * 1024 * 1024,
            ),
        )(
            depths.T,
            widths.T,
            labels,
            patches,
            gains,
            token_first,
            token_second,
            channel_first,
            channel_second,
            final_gain[None, :],
            head_weight.T,
        )
        return line[0, :candidates]

    return jax.shard_map(
        local,
        mesh=mesh,
        in_specs=(
            P("ba", None, None),
            P("aa", None, None),
            P("aa", None, None),
            P("aa", None, None),
            P("aa", None, None),
            P("aa", None, None),
            P(),
            P(),
            P(),
            P(),
            P("ba"),
        ),
        out_specs=P(),
        check_vma=False,
    )
```
